256 devices in a mesh: gx: 4 (over z_lo), gy: 4 (over x), gz: 16 (over y, z_hi, core).
Axes of the slice: x: 4, y: 4, z: 8 (z_hi: 2, z_lo: 4; z = z_hi * 4 + z_lo), core: 2. Of those that a mesh axis runs over, the one named last changes fastest.
Arguments:
- features: bfloat16 [8, 16, 16, 128, 256], P('gx', 'gy', 'gz'), may hold values from -6 to 6
- fractions: bfloat16 [8, 16, 16, 3, 128], P('gx', 'gy', 'gz'), may hold values from 0 to 0.98828125
- occupied: int32 [8, 16, 16, 128], P('gx', 'gy', 'gz'), may hold values 0 or 1
- wave_index: int32 [3, 512], replicated, may hold values from -14 to 14, as said below
- radial_weight: float32 [8, 4], replicated, may hold values from -4 to 4
- ewald_mix: float32 [256, 256], replicated, may hold values from -0.375 to 0.375
- msg_weight: bfloat16 [256, 256], replicated, may hold values from -0.375 to 0.375
- ewald_weight: bfloat16 [256, 256], replicated, may hold values from -0.375 to 0.375
- out_weight: bfloat16 [256, 256], replicated, may hold values from -0.375 to 0.375
Outputs:
- updated: bfloat16 [8, 16, 16, 128, 256], P('gx', 'gy', 'gz')
The draws below stay inside these ranges and needn't reach their ends.
Inputs may be any that keep to these rules, and one draw needn't show every extreme that they name: `wave_index`: no wavevector is zero, and no two wavevectors are equal or opposite.
All inputs are finite; a program needn't handle non-finite values. No bound on the sum of `occupied` on one device may be relied on, other than what follows from the above.
Results may differ from the reference program's by a relative error of at most 0.007.
Values may be sent and summed in bfloat16 or wider, within the bound.
No kernel may reach another device: no remote copies, remote signals or barrier semaphores. Data moves between devices by JAX's collectives and lax.ppermute only.
A program may use at most 64 MiB of HBM per device.

```python
import math
import jax
import jax.numpy as jnp
from jax import lax

FEAT = 256
WAVES = 512
SLOTS = 128
HEADS = 4
BASIS = 8
NXC = 8
NYC = 16
NZC = 16
ATOMS = 262144


def draw_wave_index(key, part):
    reach_x = NXC // 2 + 6
    reach_y = NYC // 2 + 6
    reach_z = NZC // 2 + 6
    longest = max(NXC, NYC, NZC)
    factor_x = (longest // NXC) ** 2
    factor_y = (longest // NYC) ** 2
    factor_z = (longest // NZC) ** 2
    comp_x, comp_y, comp_z = jnp.meshgrid(jnp.arange(-reach_x, reach_x + 1, dtype=jnp.int32), jnp.arange(-reach_y, reach_y + 1, dtype=jnp.int32), jnp.arange(-reach_z, reach_z + 1, dtype=jnp.int32), indexing='ij')
    comp_x = comp_x.reshape(-1)
    comp_y = comp_y.reshape(-1)
    comp_z = comp_z.reshape(-1)
    upper = (comp_x > 0) | (comp_x == 0) & (comp_y > 0) | (comp_x == 0) & (comp_y == 0) & (comp_z > 0)
    norm_int = comp_x * comp_x * factor_x + comp_y * comp_y * factor_y + comp_z * comp_z * factor_z
    score = jnp.where(upper, norm_int, jnp.int32(2 ** 30))
    pool_count = score.shape[0]
    shuffled = jax.random.permutation(jax.random.fold_in(key, 31), pool_count).astype(jnp.int32)
    ranked = jnp.argsort(score[shuffled], stable=True)
    lowest = shuffled[ranked[:2 * WAVES]]
    picks = jax.random.permutation(jax.random.fold_in(key, 37), 2 * WAVES)[:WAVES]
    chosen = lowest[picks]
    signs = 2 * jax.random.randint(jax.random.fold_in(key, 41), (WAVES,), 0, 2) - 1
    values = jnp.stack([comp_x[chosen], comp_y[chosen], comp_z[chosen]], axis=0) * signs[None, :]
    return values.astype(jnp.int32)


def place_ends(entries, key, least, high):
    index_at = [jax.random.randint(jax.random.fold_in(key, axis), (), 0, length) for axis, length in enumerate(entries.shape)]
    widest = entries.shape.index(max(entries.shape))
    next_to = index_at[:widest] + [(index_at[widest] + 1) % entries.shape[widest]] + index_at[widest + 1:]
    return entries.at[tuple(index_at)].set(least).at[tuple(next_to)].set(high)


def steps_of(stream_key, shape, shards, least, high):
    loudness, own = 1.0, jax.random.fold_in(stream_key, 6)
    for position, blocks in shards:
        steps = jnp.exp(jax.random.uniform(jax.random.fold_in(own, position), (blocks,), jnp.float32, least / len(shards), high / len(shards)))
        loudness = loudness * jnp.repeat(steps, shape[position] // blocks).reshape([-1 if axis == position else 1 for axis in range(len(shape))])
    return loudness


def noise(rng, dims, scale, bound, cuts=(), kind=jnp.bfloat16):
    values = jax.random.normal(rng, dims, jnp.float32) * scale
    if len(cuts) > 0:
        values = steps_of(rng, dims, cuts, -0.22, 0.18) * values
    return jnp.clip(values, min=-bound, max=bound).astype(kind)


def setup_inputs(seed: int = 0) -> dict:
    key_of = jax.random.split(jax.random.key(seed), 10)
    return {
        "features": noise(key_of[0], (NXC, NYC, NZC, SLOTS, FEAT), 1.0, 6.0, ((0, 4), (1, 4), (2, 16))),
        "fractions": jnp.clip(0.98828125 * jax.random.uniform(key_of[1], (NXC, NYC, NZC, 3, SLOTS), jnp.float32) ** steps_of(key_of[1], (NXC, NYC, NZC, 3, SLOTS), ((0, 4), (1, 4), (2, 16)), -0.2, 0.2), 0.0, 0.98828125).astype(jnp.bfloat16),
        "occupied": place_ends((jax.random.randint(key_of[2], (NXC, NYC, NZC, SLOTS), 0, 8) < 7).astype(jnp.int32), jax.random.fold_in(key_of[2], 1), 0, 1),
        "wave_index": draw_wave_index(jax.random.fold_in(key_of[9], 71), 0),
        "radial_weight": noise(key_of[4], (BASIS, HEADS), 1.0, 4.0, (), jnp.float32),
        "ewald_mix": noise(key_of[5], (FEAT, FEAT), FEAT ** -0.5, 0.375, (), jnp.float32),
        "msg_weight": noise(key_of[6], (FEAT, FEAT), FEAT ** -0.5, 0.375),
        "ewald_weight": noise(key_of[7], (FEAT, FEAT), FEAT ** -0.5, 0.375),
        "out_weight": noise(key_of[8], (FEAT, FEAT), FEAT ** -0.5, 0.375),
    }


sharpness = 16.0
smearing = 0.04
screening = 4.0
strength = 24.0

def pair_weights(home_geom, near_geom, shift_vec, radial_weight, self_pair):
    slot_count = home_geom.shape[2]
    dist_sq = jnp.zeros((home_geom.shape[0], slot_count, slot_count), jnp.float32)
    for axis_id in range(3):
        axis_gap = near_geom[:, axis_id, None, :] + shift_vec[axis_id] - home_geom[:, axis_id, :, None]
        dist_sq = dist_sq + axis_gap * axis_gap
    distance = jnp.sqrt(dist_sq)
    envelope = jnp.square(jnp.maximum(1.0 - dist_sq, 0.0)) * near_geom[:, 3, None, :]
    envelope = envelope * (1.0 - self_pair * jnp.eye(slot_count, dtype=jnp.float32))
    level_count = radial_weight.shape[0]
    radial_sum = jnp.zeros((home_geom.shape[0], radial_weight.shape[1], slot_count, slot_count), jnp.float32)
    for level_id in range(level_count):
        radial_bump = jnp.exp(-sharpness * jnp.square(distance - level_id / (level_count - 1)))
        radial_sum = radial_sum + radial_bump[:, None] * radial_weight[level_id][None, :, None, None]
    return (radial_sum * envelope[:, None]).astype(jnp.bfloat16)

def reference(features, fractions, occupied, wave_index, radial_weight, ewald_mix, msg_weight, ewald_weight, out_weight):
    head_count = radial_weight.shape[1]
    head_width = FEAT // head_count
    plane_cells = NYC * NZC
    geometry = jnp.concatenate([fractions.astype(jnp.float32), occupied[:, :, :, None, :].astype(jnp.float32)], axis=3)
    padding = ((1, 1), (1, 1), (1, 1), (0, 0), (0, 0))
    wide_feat = jnp.pad(features, padding, mode='wrap')
    wide_geom = jnp.pad(geometry, padding, mode='wrap')
    msg_scale = 1.0 / math.sqrt(4.0 * SLOTS)
    planes = jnp.arange(NXC, dtype=jnp.int32)

    def neighbour_plane(plane_id):
        feat_slab = lax.dynamic_slice_in_dim(wide_feat, plane_id, 3, 0)
        geom_slab = lax.dynamic_slice_in_dim(wide_geom, plane_id, 3, 0)
        home_geom = lax.dynamic_index_in_dim(geometry, plane_id, 0, keepdims=False).reshape(plane_cells, 4, SLOTS)
        msg_sum = jnp.zeros((plane_cells, SLOTS, head_count, head_width), jnp.float32)
        for offset_id in range(27):
            step_x = offset_id // 9 - 1
            step_y = offset_id // 3 % 3 - 1
            step_z = offset_id % 3 - 1
            near_feat = feat_slab[step_x + 1, step_y + 1:step_y + 1 + NYC, step_z + 1:step_z + 1 + NZC]
            near_feat = near_feat.reshape(plane_cells, SLOTS, head_count, head_width)
            near_geom = geom_slab[step_x + 1, step_y + 1:step_y + 1 + NYC, step_z + 1:step_z + 1 + NZC]
            near_geom = near_geom.reshape(plane_cells, 4, SLOTS)
            shift_vec = jnp.array([step_x, step_y, step_z], jnp.float32)
            self_pair = 1.0 if offset_id == 13 else 0.0
            weights = pair_weights(home_geom, near_geom, shift_vec, radial_weight, self_pair)
            msg_sum = msg_sum + jnp.einsum('nhpq,nqhc->nphc', weights.astype(jnp.float32), near_feat.astype(jnp.float32))
        scaled = msg_sum.reshape(plane_cells, SLOTS, FEAT) * msg_scale
        return scaled.astype(jnp.bfloat16).reshape(NYC, NZC, SLOTS, FEAT)
    messages = lax.map(neighbour_plane, planes)
    lengths = jnp.array([NXC, NYC, NZC], jnp.float32)
    wave_vec = 2.0 * math.pi * wave_index.astype(jnp.float32) / lengths[:, None]
    wave_sq = lax.optimization_barrier(jnp.sum(wave_vec * wave_vec, axis=0))
    damping = strength * jnp.exp(-0.5 * smearing * wave_sq) / (wave_sq + screening) * (1.0 / math.sqrt(ATOMS * WAVES))
    y_cells = jnp.arange(NYC, dtype=jnp.int32).astype(jnp.float32)[:, None, None]
    z_cells = jnp.arange(NZC, dtype=jnp.int32).astype(jnp.float32)[None, :, None]

    def plane_basis(plane_id):
        slab = lax.dynamic_index_in_dim(fractions, plane_id, 0, keepdims=False).astype(jnp.float32)
        pos_x = plane_id.astype(jnp.float32) + slab[:, :, 0]
        pos_y = y_cells + slab[:, :, 1]
        pos_z = z_cells + slab[:, :, 2]
        phase_rows = pos_x[..., None] * wave_vec[0] + pos_y[..., None] * wave_vec[1] + pos_z[..., None] * wave_vec[2]
        phase_rows = phase_rows.reshape(plane_cells * SLOTS, WAVES)
        return jnp.concatenate([jnp.cos(phase_rows), jnp.sin(phase_rows)], axis=1).astype(jnp.bfloat16)

    def project(carry, plane_id):
        wave_basis = plane_basis(plane_id)
        plane_feat = lax.dynamic_index_in_dim(features, plane_id, 0, keepdims=False)
        plane_mask = lax.dynamic_index_in_dim(occupied, plane_id, 0, keepdims=False)
        masked = (plane_feat * plane_mask[..., None].astype(jnp.bfloat16)).reshape(plane_cells * SLOTS, FEAT)
        term = lax.dot_general(wave_basis, masked, (((0,), (0,)), ((), ())), preferred_element_type=jnp.float32)
        return (carry + term, None)
    structure, unused = lax.scan(project, jnp.zeros((2 * WAVES, FEAT), jnp.float32), planes)
    mixed_rows = jnp.dot(structure, ewald_mix, precision=lax.Precision.HIGHEST).reshape(2, WAVES, FEAT)
    filtered = (mixed_rows * damping[None, :, None]).astype(jnp.bfloat16).reshape(2 * WAVES, FEAT)

    def decode(plane_id):
        values = jnp.dot(plane_basis(plane_id), filtered, preferred_element_type=jnp.float32)
        return values.astype(jnp.bfloat16).reshape(NYC, NZC, SLOTS, FEAT)
    ewald_out = lax.map(decode, planes)
    msg_rows = messages.reshape(-1, FEAT)
    ewald_rows = ewald_out.reshape(-1, FEAT)
    joined = jnp.dot(msg_rows, msg_weight, preferred_element_type=jnp.float32) + jnp.dot(ewald_rows, ewald_weight, preferred_element_type=jnp.float32)
    hidden = jax.nn.silu(joined).astype(jnp.bfloat16)
    result = features.reshape(-1, FEAT).astype(jnp.float32) + jnp.dot(hidden, out_weight, preferred_element_type=jnp.float32)
    result = result * occupied.reshape(-1, 1).astype(jnp.float32)
    return result.astype(jnp.bfloat16).reshape(features.shape)
```

```python
import math

import jax
import jax.numpy as jnp
from jax import lax
from jax.experimental import pallas as pl
from jax.experimental.pallas import tpu as pltpu
from jax.sharding import PartitionSpec as P

sharpness = 16.0
smearing = 0.04
screening = 4.0
strength = 24.0
BF = jnp.bfloat16
F32 = jnp.float32
LOG2E = 1.4426950408889634
REACH_SQ = sharpness * LOG2E
SCALE = math.sqrt(REACH_SQ)
FAR_AWAY = 1000.0
LEVELS = 8
STEP = 1.0 / (LEVELS - 1)
POWER = 2.0 * sharpness * STEP * LOG2E / SCALE
VMEM = 56 * 1024 * 1024


def bumps(home, row, shift, eye):
    dist_sq = None
    for a in range(3):
        gap = (row[a] + shift[a]) - home[a]
        dist_sq = gap * gap if dist_sq is None else dist_sq + gap * gap
    dist_sq = jnp.minimum(dist_sq, REACH_SQ)
    if eye is not None:
        dist_sq = jnp.where(eye, REACH_SQ, dist_sq)
    rise = REACH_SQ - dist_sq
    distance = dist_sq * lax.rsqrt(jnp.maximum(dist_sq, 1e-30))
    ratio = jnp.exp2(POWER * distance)
    value = rise * rise * jnp.exp2(-dist_sq)
    values = [value]
    for _ in range(LEVELS - 1):
        value = value * ratio
        values.append(value)
    return values


def pair_kernel(own, first, *refs):
    if first:
        feat_ref, row_ref, home_ref, weight_ref, acc_ref, y_ref, fw_ref = refs
    else:
        feat_ref, row_ref, home_ref, weight_ref, old_ref, acc_ref, y_ref, fw_ref = refs
    source = pl.program_id(0)
    sx = source // 4
    sy = source % 4

    @pl.when(source == 0)
    def _():
        if first:
            acc_ref[...] = jnp.zeros_like(acc_ref)
        else:
            acc_ref[...] = old_ref[...]

    feat = feat_ref[0].astype(F32)
    for b in range(LEVELS):
        fw_ref[b * 128 : (b + 1) * 128, :] = (feat * weight_ref[b : b + 1, :]).astype(BF)
    row = [row_ref[0, a : a + 1, :] for a in range(3)]
    rows = 32
    for j in range(9):
        jx, jy = j // 3, j % 3
        cell = (sx + jx) * 6 + sy + jy
        shift = ((1 - jx) * SCALE, (1 - jy) * SCALE, 0.0)
        for r in range(128 // rows):
            cols = home_ref[cell, r * rows : (r + 1) * rows, :]
            home = [cols[:, a : a + 1] for a in range(3)]
            eye = None
            if own and j == 4:
                eye = lax.broadcasted_iota(jnp.int32, (rows, 128), 0) + r * rows == (
                    lax.broadcasted_iota(jnp.int32, (rows, 128), 1)
                )
            values = bumps(home, row, shift, eye)
            for b in range(LEVELS):
                y_ref[j * 128 + r * rows : j * 128 + (r + 1) * rows, b * 128 : (b + 1) * 128] = (
                    values[b].astype(BF)
                )
    out = jnp.dot(y_ref[...], fw_ref[...], preferred_element_type=F32)
    for j in range(9):
        cell = (sx + j // 3) * 6 + sy + j % 3
        acc_ref[cell] += out[j * 128 : (j + 1) * 128]


def pair_messages(feat, row, home, weight, old, own, name):
    first = old is None
    whole = pl.BlockSpec((24, 128, 256), lambda s: (0, 0, 0))
    in_specs = [
        pl.BlockSpec((1, 128, 256), lambda s: (s, 0, 0)),
        pl.BlockSpec((1, 8, 128), lambda s: (s, 0, 0)),
        pl.BlockSpec((24, 128, 8), lambda s: (0, 0, 0)),
        pl.BlockSpec((8, 256), lambda s: (0, 0)),
    ]
    args = [feat, row, home, weight]
    aliases = {}
    if not first:
        in_specs.append(whole)
        args.append(old)
        aliases = {4: 0}

    def kernel(*refs):
        pair_kernel(own, first, *refs)

    return pl.pallas_call(
        kernel,
        grid=(8,),
        in_specs=in_specs,
        out_specs=whole,
        out_shape=jax.ShapeDtypeStruct((24, 128, 256), F32),
        scratch_shapes=[pltpu.VMEM((1152, 1024), BF), pltpu.VMEM((1024, 256), BF)],
        input_output_aliases=aliases,
        compiler_params=pltpu.CompilerParams(
            dimension_semantics=("arbitrary",), vmem_limit_bytes=VMEM
        ),
        name=name,
    )(*args)


SIN = [
    math.pi * (-1) ** i * math.pi ** (2 * i) / math.factorial(2 * i + 1) for i in range(7)
]
COS = [(-1) ** i * math.pi ** (2 * i) / math.factorial(2 * i) for i in range(7)]


def cos_sin(turns):
    part = turns - jnp.floor(turns + 0.5)
    sq = part * part
    sin_half = jnp.full_like(sq, SIN[-1])
    cos_half = jnp.full_like(sq, COS[-1])
    for i in range(len(SIN) - 2, -1, -1):
        sin_half = sin_half * sq + SIN[i]
        cos_half = cos_half * sq + COS[i]
    sin_half = sin_half * part
    twice = sin_half + sin_half
    return 1.0 - twice * sin_half, twice * cos_half


def structure_kernel(feat_ref, row_ref, wave_ref, out_ref, bt_ref):
    for c in range(16):
        waves = wave_ref[c * 32 : (c + 1) * 32, :]
        wave = [jnp.broadcast_to(waves[:, a : a + 1], (32, 128)) for a in range(3)]
        for n in range(8):
            turns = None
            for a in range(3):
                term = wave[a] * row_ref[n, 4 + a : 5 + a, :]
                turns = term if turns is None else turns + term
            cos, sin = cos_sin(turns)
            mask = row_ref[n, 3:4, :]
            bt_ref[c * 64 : c * 64 + 32, n * 128 : (n + 1) * 128] = (cos * mask).astype(BF)
            bt_ref[c * 64 + 32 : c * 64 + 64, n * 128 : (n + 1) * 128] = (sin * mask).astype(BF)
    out_ref[...] = jnp.dot(bt_ref[...], feat_ref[...], preferred_element_type=F32).astype(BF)


def structure(feat, row, wave_cols):
    return pl.pallas_call(
        structure_kernel,
        out_shape=jax.ShapeDtypeStruct((1024, 256), BF),
        scratch_shapes=[pltpu.VMEM((1024, 1024), BF)],
        compiler_params=pltpu.CompilerParams(vmem_limit_bytes=VMEM),
        name="structure",
    )(feat, row, wave_cols)


def basis_kernel(home_ref, wave_ref, out_ref):
    for r in range(4):
        cols = home_ref[0, r * 32 : (r + 1) * 32, :]
        place = [jnp.broadcast_to(cols[:, 4 + a : 5 + a], (32, 128)) for a in range(3)]
        for c in range(4):
            turns = None
            for a in range(3):
                term = place[a] * wave_ref[a : a + 1, c * 128 : (c + 1) * 128]
                turns = term if turns is None else turns + term
            cos, sin = cos_sin(turns)
            out_ref[r * 32 : (r + 1) * 32, c * 256 : c * 256 + 128] = cos.astype(BF)
            out_ref[r * 32 : (r + 1) * 32, c * 256 + 128 : c * 256 + 256] = sin.astype(BF)


def basis(home, wave_rows):
    return pl.pallas_call(
        basis_kernel,
        grid=(8,),
        in_specs=[
            pl.BlockSpec((1, 128, 8), lambda n: ((n // 4 + 1) * 6 + n % 4 + 1, 0, 0)),
            pl.BlockSpec((8, 512), lambda n: (0, 0)),
        ],
        out_specs=pl.BlockSpec((128, 1024), lambda n: (n, 0)),
        out_shape=jax.ShapeDtypeStruct((1024, 1024), BF),
        compiler_params=pltpu.CompilerParams(vmem_limit_bytes=VMEM),
        name="wave_basis",
    )(home, wave_rows)


def update_kernel(
    basis_ref, f0, f1, f2, f3, acc_ref, y0, y3, x0, x1, feat_ref, home_ref, mw, ew, ow, out_ref
):
    half = pl.program_id(0)
    values = None
    for i, f in enumerate((f0, f1, f2, f3)):
        part = jnp.dot(
            basis_ref[:, i * 256 : (i + 1) * 256], f[...], preferred_element_type=F32
        )
        values = part if values is None else values + part
    ewald = values.astype(BF)
    cells = []
    for y in range(4):
        total = acc_ref[0, y + 1]
        if y == 0:
            total = total + y0[0].astype(F32)
        if y == 3:
            total = total + y3[0].astype(F32)
        total = total + jnp.where(half == 0, x0[y].astype(F32), x1[y].astype(F32))
        cells.append(total.astype(BF))
    messages = jnp.concatenate(cells, axis=0)
    joined = jnp.dot(messages, mw[...], preferred_element_type=F32) + jnp.dot(
        ewald, ew[...], preferred_element_type=F32
    )
    hidden = (joined / (1.0 + jnp.exp(-joined))).astype(BF)
    update = jnp.dot(hidden, ow[...], preferred_element_type=F32)
    for y in range(4):
        rows = slice(y * 128, (y + 1) * 128)
        mask = home_ref[0, y + 1, :, 3:4]
        out_ref[y] = ((feat_ref[y].astype(F32) + update[rows]) * mask).astype(BF)


def update(base, filt, acc, y_low, y_high, x_low, x_high, feat, home, mw, ew, ow):
    full = lambda shape: pl.BlockSpec(shape, lambda i: (0,) * len(shape))
    return pl.pallas_call(
        update_kernel,
        grid=(2,),
        in_specs=[
            pl.BlockSpec((512, 1024), lambda i: (i, 0)),
            full((256, 256)),
            full((256, 256)),
            full((256, 256)),
            full((256, 256)),
            pl.BlockSpec((1, 6, 128, 256), lambda i: (i + 1, 0, 0, 0)),
            pl.BlockSpec((1, 128, 256), lambda i: (i + 1, 0, 0)),
            pl.BlockSpec((1, 128, 256), lambda i: (i + 1, 0, 0)),
            full((4, 128, 256)),
            full((4, 128, 256)),
            pl.BlockSpec((4, 128, 256), lambda i: (i, 0, 0)),
            pl.BlockSpec((1, 6, 128, 8), lambda i: (i + 1, 0, 0, 0)),
            full((256, 256)),
            full((256, 256)),
            full((256, 256)),
        ],
        out_specs=pl.BlockSpec((4, 128, 256), lambda i: (i, 0, 0)),
        out_shape=jax.ShapeDtypeStruct((8, 128, 256), BF),
        compiler_params=pltpu.CompilerParams(vmem_limit_bytes=VMEM),
        name="update",
    )(
        base,
        *filt,
        acc.reshape(4, 6, 128, 256),
        y_low,
        y_high,
        x_low,
        x_high,
        feat,
        home.reshape(4, 6, 128, 8),
        mw,
        ew,
        ow,
    )


def shifted(count, step):
    return [(i, (i + step) % count) for i in range(count)]


def high_digit(step):
    return [(i, (i // 4 + step) % 4 * 4 + i % 4) for i in range(16)]


def low_digit(step):
    return [(i, i ^ step) for i in range(16)]


def far_pairs():
    return [(i, (i + 1) % 16 if i % 2 else (i - 1) % 16) for i in range(16)]


def body(
    features,
    fractions,
    occupied,
    wave_index,
    radial_weight,
    ewald_mix,
    msg_weight,
    ewald_weight,
    out_weight,
):
    gx, gy, gz = (lax.axis_index(name) for name in ("gx", "gy", "gz"))
    feat = features.reshape(8, 128, 256)
    frac = fractions.reshape(2, 4, 3, 128)
    mask = occupied.reshape(8, 1, 128).astype(BF)
    geometry = jnp.concatenate([frac.reshape(8, 3, 128), mask], axis=1)

    near_geom = lax.ppermute(geometry, "gz", low_digit(1))
    near_feat = lax.ppermute(feat, "gz", low_digit(1))
    far_geom = lax.ppermute(geometry, "gz", far_pairs())
    far_feat = lax.ppermute(feat, "gz", far_pairs())

    left = lax.ppermute(frac[1:], "gx", shifted(4, 1))
    right = lax.ppermute(frac[:1], "gx", shifted(4, -1))
    wide = jnp.concatenate([left, frac, right], axis=0)
    below = lax.ppermute(wide[:, 3:], "gy", shifted(4, 1))
    above = lax.ppermute(wide[:, :1], "gy", shifted(4, -1))
    wide = jnp.concatenate([below, wide, above], axis=1)

    occ = mask.astype(F32)
    starts = jnp.stack(
        [
            jnp.broadcast_to((gx * 2 + jnp.arange(2))[:, None], (2, 4)),
            jnp.broadcast_to((gy * 4 + jnp.arange(4))[None, :], (2, 4)),
            jnp.broadcast_to(gz, (2, 4)),
        ],
        axis=-1,
    ).astype(F32)
    lengths = jnp.array([8.0, 16.0, 16.0], F32)
    place = (starts[..., None] + frac.astype(F32)) / lengths[:, None]

    def source_rows(geom, lift):
        pos = geom[:, :3].astype(F32) * SCALE
        hide = (1.0 - geom[:, 3:].astype(F32)) * FAR_AWAY
        return jnp.concatenate(
            [pos[:, :1] + hide, pos[:, 1:2], pos[:, 2:] + lift * SCALE, geom[:, 3:].astype(F32)],
            axis=1,
        )

    core_sign = 1.0 - 2.0 * (gz % 2).astype(F32)
    own_rows = jnp.concatenate(
        [source_rows(geometry, 0.0), place.reshape(8, 3, 128), jnp.zeros((8, 1, 128), F32)], axis=1
    )
    pad_rows = lambda rows: jnp.concatenate([rows, jnp.zeros((8, 4, 128), F32)], axis=1)
    near_rows = pad_rows(source_rows(near_geom, core_sign))
    far_rows = pad_rows(source_rows(far_geom, -core_sign))

    own_extra = jnp.concatenate(
        [occ.reshape(2, 4, 1, 128), place, jnp.zeros((2, 4, 1, 128), F32)], axis=2
    )
    own_extra = jnp.pad(own_extra, ((1, 1), (1, 1), (0, 0), (0, 0)))
    home = jnp.concatenate([wide.astype(F32) * SCALE, own_extra], axis=2)
    home = home.reshape(24, 8, 128).transpose(0, 2, 1)

    level = jnp.arange(LEVELS, dtype=F32)[:, None] * STEP
    weight = radial_weight * jnp.exp(-sharpness * level * level)
    weight = weight * (1.0 / (REACH_SQ * REACH_SQ * math.sqrt(512.0)))
    weight = jnp.repeat(weight, 64, axis=1)

    blocks = wave_index.astype(F32).reshape(3, 4, 4, 32)

    def turned(values, axis, start):
        twice = jnp.concatenate([values, values], axis=axis)
        return lax.dynamic_slice_in_dim(twice, start, 4, axis=axis)

    sent = turned(turned(blocks, 1, gy), 2, gx)
    wave_cols = jnp.pad(sent.reshape(3, 512).T, ((0, 0), (0, 5)))
    come = turned(turned(blocks[:, ::-1, ::-1], 1, 3 - gy), 2, 3 - gx)
    wave_rows = jnp.pad(come.reshape(3, 512), ((0, 5), (0, 0)))

    terms = structure(feat.reshape(1024, 256), own_rows, wave_cols).reshape(4, 256, 256)
    got = [lax.ppermute(terms[s], "gy", shifted(4, s)) for s in (1, 2, 3)]
    acc = pair_messages(feat, own_rows, home, weight, None, True, "pair_own")
    sums = terms[0].astype(F32) + got[0].astype(F32) + got[1].astype(F32) + got[2].astype(F32)
    sums = sums.astype(BF).reshape(4, 64, 256)
    got = [lax.ppermute(sums[r], "gx", shifted(4, r)) for r in (1, 2, 3)]
    acc = pair_messages(near_feat, near_rows, home, weight, acc, False, "pair_near")
    sums = sums[0].astype(F32) + got[0].astype(F32) + got[1].astype(F32) + got[2].astype(F32)
    sent_sums = sums.astype(BF)
    got = [lax.ppermute(sent_sums, "gz", high_digit(s)) for s in (1, 2, 3)]
    sums = sums + got[0].astype(F32) + got[1].astype(F32) + got[2].astype(F32)
    sent_sums = sums.astype(BF)
    got = [lax.ppermute(sent_sums, "gz", low_digit(s)) for s in (1, 2, 3)]
    sums = sums + got[0].astype(F32) + got[1].astype(F32) + got[2].astype(F32)

    wave_vec = 2.0 * math.pi * sent[:, 0, 0] / lengths[:, None]
    wave_sq = jnp.sum(wave_vec * wave_vec, axis=0)
    damping = (
        strength
        * jnp.exp(-0.5 * smearing * wave_sq)
        / (wave_sq + screening)
        * (1.0 / math.sqrt(262144 * 512))
    )
    mixed = jnp.dot(sums, ewald_mix, precision=lax.Precision.HIGHEST)
    filtered = (mixed.reshape(2, 32, 256) * damping[None, :, None]).astype(BF)
    filtered = [filtered] + [lax.ppermute(filtered, "gx", shifted(4, r)) for r in (1, 2, 3)]
    filtered = jnp.stack(filtered, axis=1).reshape(256, 256)
    filtered = [filtered] + [lax.ppermute(filtered, "gy", shifted(4, s)) for s in (1, 2, 3)]

    base = basis(home, wave_rows)
    acc = pair_messages(far_feat, far_rows, home, weight, acc, False, "pair_far")
    wide_acc = acc.reshape(4, 6, 128, 256)
    y_high = lax.ppermute(wide_acc[:, 0].astype(BF), "gy", shifted(4, -1))
    y_low = lax.ppermute(wide_acc[:, 5].astype(BF), "gy", shifted(4, 1))

    def edge(x):
        cells = [wide_acc[x, 1] + y_low[x].astype(F32), wide_acc[x, 2]]
        cells += [wide_acc[x, 3], wide_acc[x, 4] + y_high[x].astype(F32)]
        return jnp.stack(cells).astype(BF)

    x_high = lax.ppermute(edge(0), "gx", shifted(4, -1))
    x_low = lax.ppermute(edge(3), "gx", shifted(4, 1))
    out = update(
        base,
        filtered,
        acc,
        y_low,
        y_high,
        x_low,
        x_high,
        feat,
        home,
        msg_weight,
        ewald_weight,
        out_weight,
    )
    return out.reshape(features.shape)


def solution(mesh):
    in_specs = (
        P("gx", "gy", "gz", None, None),
        P("gx", "gy", "gz", None, None),
        P("gx", "gy", "gz", None),
        P(),
        P(),
        P(),
        P(),
        P(),
        P(),
    )
    out_specs = P("gx", "gy", "gz", None, None)
    return jax.shard_map(body, mesh=mesh, in_specs=in_specs, out_specs=out_specs, check_vma=False)
```

```python
import math

import jax
import jax.numpy as jnp
from jax import lax
from jax.experimental import pallas as pl
from jax.experimental.pallas import tpu as pltpu
from jax.sharding import PartitionSpec as P

sharpness = 16.0
smearing = 0.04
screening = 4.0
strength = 24.0
BF = jnp.bfloat16
F32 = jnp.float32
LOG2E = 1.4426950408889634
REACH_SQ = sharpness * LOG2E
SCALE = math.sqrt(REACH_SQ)
FAR_AWAY = 1000.0
LEVELS = 8
LENGTHS = (8.0, 16.0, 16.0)
STEP = 1.0 / (LEVELS - 1)
POWER = 2.0 * sharpness * STEP * LOG2E / SCALE


def vmem():
    return pl.BlockSpec(memory_space=pltpu.VMEM)


def smem():
    return pl.BlockSpec(memory_space=pltpu.SMEM)


def call(kernel, name, outs, args, scratch=(), scalars=0, mega=8):
    return pl.pallas_call(
        kernel,
        in_specs=[smem()] * scalars + [vmem()] * (len(args) - scalars),
        out_specs=tuple(vmem() for _ in outs),
        out_shape=tuple(jax.ShapeDtypeStruct(shape, dtype) for shape, dtype in outs),
        scratch_shapes=[pltpu.VMEM(shape, dtype) for shape, dtype in scratch],
        compiler_params=pltpu.CompilerParams(vmem_limit_bytes=mega * 1024 * 1024),
        name=name,
    )(*args)


def prepare_kernel(
    feat_ref, frac_ref, occ_ref, wave_ref, radial_ref, pay_ref, cols_ref, weight_ref, own_ref
):
    for n in range(8):
        pay_ref[n, 0:128, :] = feat_ref[n]
        geom = jnp.concatenate(
            [frac_ref[n].astype(F32), occ_ref[n].astype(F32), jnp.zeros((4, 128), F32)], axis=0
        )
        own_ref[n] = geom.T
        wide = jnp.concatenate([geom, jnp.zeros((8, 128), F32)], axis=1)
        pay_ref[n, 128:136, :] = wide.astype(BF)
    waves = jnp.concatenate([wave_ref[...].astype(F32), jnp.zeros((5, 512), F32)], axis=0)
    for c in range(4):
        cols_ref[c * 128 : (c + 1) * 128, :] = waves[:, c * 128 : (c + 1) * 128].T
    level = lax.broadcasted_iota(jnp.int32, (8, 256), 0).astype(F32) * STEP
    lane = lax.broadcasted_iota(jnp.int32, (8, 256), 1)
    radial = jnp.broadcast_to(radial_ref[:, 3:4], (8, 256))
    for h in (2, 1, 0):
        radial = jnp.where(lane < 64 * (h + 1), radial_ref[:, h : h + 1], radial)
    fixed = 1.0 / (REACH_SQ * REACH_SQ * math.sqrt(512.0))
    weight_ref[...] = radial * (jnp.exp(-sharpness * level * level) * fixed)


SIN = [
    math.pi * (-1) ** i * math.pi ** (2 * i) / math.factorial(2 * i + 1) for i in range(7)
]
COS = [(-1) ** i * math.pi ** (2 * i) / math.factorial(2 * i) for i in range(7)]


def cos_sin(turns):
    part = turns - jnp.floor(turns + 0.5)
    sq = part * part
    sin_half = jnp.full_like(sq, SIN[-1])
    cos_half = jnp.full_like(sq, COS[-1])
    for i in range(len(SIN) - 2, -1, -1):
        sin_half = sin_half * sq + SIN[i]
        cos_half = cos_half * sq + COS[i]
    sin_half = sin_half * part
    twice = sin_half + sin_half
    return 1.0 - twice * sin_half, twice * cos_half


def structure_kernel(where_ref, pay_ref, cols_ref, t0, t1, t2, t3, bt_ref, mask_ref, total_ref):
    places = []
    starts = [where_ref[0] * 2, where_ref[1] * 4, where_ref[2]]
    for n in range(8):
        geom = pay_ref[n, 128:136, 0:128].astype(F32)
        cell = [starts[0] + n // 4, starts[1] + n % 4, starts[2]]
        places.append(
            [(cell[a].astype(F32) + geom[a : a + 1]) * (1.0 / LENGTHS[a]) for a in range(3)]
        )
        mask_ref[n : n + 1, :] = geom[3:4]
    for c in range(16):
        waves = cols_ref[c * 32 : (c + 1) * 32, :]
        wave = [jnp.broadcast_to(waves[:, a : a + 1], (32, 128)) for a in range(3)]
        for n in range(8):
            turns = None
            for a in range(3):
                term = wave[a] * places[n][a]
                turns = term if turns is None else turns + term
            cos, sin = cos_sin(turns)
            mask = mask_ref[n : n + 1, :]
            bt_ref[c * 64 : c * 64 + 32, n * 128 : (n + 1) * 128] = (cos * mask).astype(BF)
            bt_ref[c * 64 + 32 : c * 64 + 64, n * 128 : (n + 1) * 128] = (sin * mask).astype(BF)
    feat = jnp.concatenate([pay_ref[n, 0:128, :] for n in range(8)], axis=0)
    total_ref[...] = jnp.dot(bt_ref[...], feat, preferred_element_type=F32)
    for s, out in enumerate((t0, t1, t2, t3)):
        for r in range(4):
            start = ((where_ref[1] + s) % 4) * 256 + ((where_ref[0] + r) % 4) * 64
            rows = total_ref[pl.ds(pl.multiple_of(start, 64), 64), :]
            out[r * 64 : (r + 1) * 64, :] = rows.astype(BF)
    for x in range(2):
        t1[256 + x * 8 : 264 + x * 8, :] = pay_ref[x * 4 + 3, 128:136, :]
        t3[256 + x * 8 : 264 + x * 8, :] = pay_ref[x * 4, 128:136, :]


def first_sum_kernel(t0, g1, g2, g3, pay_ref, u0, u1, u2, u3):
    for r, out in enumerate((u0, u1, u2, u3)):
        rows = slice(r * 64, (r + 1) * 64)
        total = t0[rows, :].astype(F32) + g1[rows, :].astype(F32)
        total = total + (g2[rows, :].astype(F32) + g3[rows, :].astype(F32))
        out[0:64, :] = total.astype(out.dtype)
    for x, out in ((1, u1), (0, u3)):
        out[64:72, :] = g1[256 + x * 8 : 264 + x * 8, :]
        for y in range(4):
            out[72 + y * 8 : 80 + y * 8, :] = pay_ref[x * 4 + y, 128:136, :]
        out[104:112, :] = g3[256 + x * 8 : 264 + x * 8, :]


def second_sum_kernel(u0, h1, h2, h3, g1, g3, own_ref, sum_ref, sent_ref, home_ref):
    total = u0[...] + h1[0:64, :].astype(F32) + h2[...].astype(F32) + h3[0:64, :].astype(F32)
    sum_ref[...] = total
    sent_ref[...] = total.astype(BF)
    for side, got in ((0, h1), (3, h3)):
        for y in range(6):
            block = got[64 + y * 8 : 72 + y * 8, 0:128].astype(F32)
            home_ref[side * 6 + y] = block.T
    for x in range(2):
        for y, got in ((0, g1), (5, g3)):
            block = got[256 + x * 8 : 264 + x * 8, 0:128].astype(F32)
            home_ref[(x + 1) * 6 + y] = block.T
        for y in range(4):
            home_ref[(x + 1) * 6 + y + 1] = own_ref[x * 4 + y]


def third_sum_kernel(v, a, b, c, sum_ref, sent_ref):
    total = v[...] + a[...].astype(F32) + b[...].astype(F32) + c[...].astype(F32)
    sum_ref[...] = total
    sent_ref[...] = total.astype(BF)


def filter_kernel(where_ref, w, a, b, c, mix_ref, cols_ref, low_ref, high_ref, x1, x2, x3):
    total = w[...] + a[...].astype(F32) + b[...].astype(F32) + c[...].astype(F32)
    mixed = jnp.dot(
        total, mix_ref[...], precision=lax.Precision.HIGHEST, preferred_element_type=F32
    )
    start = pl.multiple_of((where_ref[1] * 4 + where_ref[0]) * 32, 32)
    waves = cols_ref[pl.ds(start, 32), :]
    wave_sq = None
    for a in range(3):
        part = 2.0 * math.pi * waves[:, a : a + 1] / LENGTHS[a]
        wave_sq = part * part if wave_sq is None else wave_sq + part * part
    damping = strength * jnp.exp(-0.5 * smearing * wave_sq) / (wave_sq + screening)
    damping = damping * (1.0 / math.sqrt(262144 * 512))
    for half in range(2):
        rows = (mixed[half * 32 : (half + 1) * 32] * damping).astype(BF)
        x2[half * 32 : (half + 1) * 32, :] = rows
        for out in (x1, x3):
            out[768 + half * 32 : 800 + half * 32, :] = rows
    x1[0:768, :] = high_ref[...]
    x3[0:768, :] = low_ref[...]


def border_sum_kernel(yb, x0, x1, x2, x3, p1, p2, p3):
    for out, hy, side in ((p3, 0, 0), (p1, 5, 2)):
        for x, got in enumerate((x1, x3)):
            total = yb[side + x] + got[hy * 128 : (hy + 1) * 128, :].astype(F32)
            out[x * 128 : (x + 1) * 128, :] = total.astype(BF)
    for r, rows in enumerate((x0[...], x1[768:832, :], x2[...], x3[768:832, :])):
        p2[r * 64 : (r + 1) * 64, :] = rows
        for out in (p1, p3):
            out[256 + r * 64 : 320 + r * 64, :] = rows


def bumps(home, row, eye):
    dist_sq = None
    for a in range(3):
        gap = row[a] - home[a]
        dist_sq = gap * gap if dist_sq is None else dist_sq + gap * gap
    dist_sq = jnp.minimum(dist_sq, REACH_SQ)
    if eye is not None:
        dist_sq = jnp.where(eye, REACH_SQ, dist_sq)
    rise = REACH_SQ - dist_sq
    distance = dist_sq * lax.rsqrt(jnp.maximum(dist_sq, 1e-30))
    ratio = jnp.exp2(POWER * distance)
    square = ratio * ratio
    value = rise * rise * jnp.exp2(-dist_sq)
    values = [value, value * ratio]
    for b in range(2, LEVELS):
        values.append(values[b - 2] * square)
    return values


ROWS = 16
INSIDE = [(x, y) for x in (1, 2) for y in range(1, 5)]
BORDER_X = [(x, y) for x in (0, 3) for y in range(6)]
BORDER_Y = [(x, y) for y in (0, 5) for x in (1, 2)]


def pair_sums(jobs, pay_refs, lifts, home_refs, weight_ref, y_refs, fw_refs):
    groups = []
    count = 0
    for plane, homes, accumulate in jobs:
        for source in range(8):
            sx, sy = source // 4, source % 4
            near = [
                i for i, (hx, hy) in enumerate(homes) if 0 <= hx - sx <= 2 and 0 <= hy - sy <= 2
            ]
            for k in range(0, len(near), 3):
                groups.append((plane, source, homes, near[k : k + 3], accumulate, count))
            count += bool(near)

    rows_of = {}

    def fill(index):
        plane, source, homes, near, _, slot = groups[index]
        sx, sy = source // 4, source % 4
        y_ref, fw_ref = y_refs[index % 2], fw_refs[slot % 2]
        if index == 0 or groups[index - 1][5] != slot:
            feat = pay_refs[plane][source, 0:128, :].astype(F32)
            for b in range(LEVELS):
                fw_ref[b * 128 : (b + 1) * 128, :] = (feat * weight_ref[b : b + 1, :]).astype(BF)
            geom = pay_refs[plane][source, 128:136, 0:128].astype(F32)
            hide = (1.0 - geom[3:4]) * FAR_AWAY
            row = [geom[0:1] * SCALE + hide, geom[1:2] * SCALE, geom[2:3] * SCALE + lifts[plane]]
            rows_of[slot] = row
        row = rows_of[slot]
        for k, i in enumerate(near):
            hx, hy = homes[i]
            jx, jy = hx - sx, hy - sy
            moved = [row[0] + (1 - jx) * SCALE, row[1] + (1 - jy) * SCALE, row[2]]
            for r in range(0, 128, ROWS):
                cols = home_refs(hx, hy, r) * SCALE
                home = [cols[:, a : a + 1] for a in range(3)]
                eye = None
                if plane == 0 and jx == 1 and jy == 1:
                    eye = lax.broadcasted_iota(jnp.int32, (ROWS, 128), 0) + r == (
                        lax.broadcasted_iota(jnp.int32, (ROWS, 128), 1)
                    )
                at = slice(k * 128 + r, k * 128 + r + ROWS)
                for b, value in enumerate(bumps(home, moved, eye)):
                    y_ref[at, b * 128 : (b + 1) * 128] = value.astype(BF)

    def multiply(index):
        _, _, _, near, _, slot = groups[index]
        return jnp.dot(
            y_refs[index % 2][0 : len(near) * 128, :],
            fw_refs[slot % 2][...],
            preferred_element_type=F32,
        )

    def gather(index, out):
        _, _, _, near, accumulate, _ = groups[index]
        for k, i in enumerate(near):
            accumulate(i, out[k * 128 : (k + 1) * 128])

    fill(0)
    for index in range(1, len(groups)):
        out = multiply(index - 1)
        fill(index)
        gather(index - 1, out)
    gather(len(groups) - 1, multiply(len(groups) - 1))


def adder(acc_ref, start):
    seen = set()

    def accumulate(i, part):
        if i in seen:
            acc_ref[i] = acc_ref[i] + part
        else:
            seen.add(i)
            acc_ref[i] = part if start is None else start(i) + part

    return accumulate


PAIR_SCRATCH = [((384, 1024), BF)] * 2 + [((1024, 256), BF)] * 2


def own_messages(pay, own, weight, column):
    homes = [(column + 1, y) for y in range(1, 5)]

    def kernel(pay_ref, own_ref, weight_ref, out_ref, ya, yb, fa, fb):
        def home(hx, hy, r):
            return own_ref[(hx - 1) * 4 + hy - 1, r : r + ROWS, :]

        jobs = [(0, homes, adder(out_ref, None))]
        pair_sums(jobs, [pay_ref], [0.0], home, weight_ref, (ya, yb), (fa, fb))

    outs = [((4, 128, 256), F32)]
    return call(kernel, "pair_own", outs, [pay, own, weight], PAIR_SCRATCH)[0]


def side_messages(where, pay, near, home, weight):
    def kernel(where_ref, pay_ref, near_ref, home_ref, weight_ref, out_ref, ya, yb, fa, fb):
        lift = where_ref[3].astype(F32) * SCALE
        add = adder(out_ref, None)
        pair_sums(
            [(0, BORDER_X, add), (1, BORDER_X, add)],
            [pay_ref, near_ref],
            [0.0, lift],
            lambda hx, hy, r: home_ref[hx * 6 + hy, r : r + ROWS, :],
            weight_ref,
            (ya, yb),
            (fa, fb),
        )

    outs = [((12, 128, 256), F32)]
    return call(kernel, "pair_side", outs, [where, pay, near, home, weight], PAIR_SCRATCH, 1)[0]


def far_side_messages(where, far, home, weight, side):
    def kernel(where_ref, far_ref, home_ref, weight_ref, side_ref, low, high, ya, yb, fa, fb, acc):
        lift = -where_ref[3].astype(F32) * SCALE
        pair_sums(
            [(1, BORDER_X, adder(acc, lambda i: side_ref[i]))],
            [None, far_ref],
            [0.0, lift],
            lambda hx, hy, r: home_ref[hx * 6 + hy, r : r + ROWS, :],
            weight_ref,
            (ya, yb),
            (fa, fb),
        )
        for i in range(6):
            low[i * 128 : (i + 1) * 128, :] = acc[i].astype(BF)
            high[i * 128 : (i + 1) * 128, :] = acc[6 + i].astype(BF)

    outs = [((768, 256), BF)] * 2
    scratch = PAIR_SCRATCH + [((12, 128, 256), F32)]
    return call(kernel, "pair_far_side", outs, [where, far, home, weight, side], scratch, 1)


def rest_messages(where, pay, near, far, home, weight, own_low, own_high):
    def kernel(
        where_ref, pay_ref, near_ref, far_ref, home_ref, weight_ref, a, b, yb_ref, in_ref, *scratch
    ):
        lift = where_ref[3].astype(F32) * SCALE
        border = adder(yb_ref, None)
        inside = adder(in_ref, lambda i: a[i] if i < 4 else b[i - 4])
        pair_sums(
            [
                (0, BORDER_Y, border),
                (1, BORDER_Y, border),
                (2, BORDER_Y, border),
                (1, INSIDE, inside),
                (2, INSIDE, inside),
            ],
            [pay_ref, near_ref, far_ref],
            [0.0, lift, -lift],
            lambda hx, hy, r: home_ref[hx * 6 + hy, r : r + ROWS, :],
            weight_ref,
            scratch[:2],
            scratch[2:],
        )

    outs = [((4, 128, 256), F32), ((8, 128, 256), F32)]
    args = [where, pay, near, far, home, weight, own_low, own_high]
    return call(kernel, "pair_rest", outs, args, PAIR_SCRATCH, 1)


def update_kernel(
    where_ref, bt_ref, f0, q1, q2, q3, in_ref, x1, x3, pay_ref, own_ref, mw, ew, ow, out_ref, filt
):
    for s, (f, base) in enumerate(((f0, 0), (q1, 256), (q2, 0), (q3, 256))):
        for r in range(4):
            start = ((where_ref[1] - s) % 4) * 256 + ((where_ref[0] - r) % 4) * 64
            filt[pl.ds(pl.multiple_of(start, 64), 64), :] = f[base + r * 64 : base + (r + 1) * 64, :]
    flipped = lax.dot_general(
        filt[...], bt_ref[...], (((0,), (0,)), ((), ())), preferred_element_type=F32
    )
    flipped = flipped.astype(BF)
    joined = lax.dot_general(
        flipped, ew[...], (((0,), (0,)), ((), ())), preferred_element_type=F32
    )
    for x, got in enumerate((x1, x3)):
        cells = []
        for y in range(4):
            total = in_ref[x * 4 + y] + got[(y + 1) * 128 : (y + 2) * 128, :].astype(F32)
            if y == 0:
                total = total + q1[x * 128 : (x + 1) * 128, :].astype(F32)
            if y == 3:
                total = total + q3[x * 128 : (x + 1) * 128, :].astype(F32)
            cells.append(total.astype(BF))
        messages = jnp.concatenate(cells, axis=0)
        part = joined[x * 512 : (x + 1) * 512]
        part = part + jnp.dot(messages, mw[...], preferred_element_type=F32)
        hidden = (part / (1.0 + jnp.exp(-part))).astype(BF)
        change = jnp.dot(hidden, ow[...], preferred_element_type=F32)
        for y in range(4):
            mask = own_ref[x * 4 + y, :, 3:4]
            feat = pay_ref[x * 4 + y, 0:128, :].astype(F32)
            out_ref[x * 4 + y] = ((feat + change[y * 128 : (y + 1) * 128]) * mask).astype(BF)


def shifted(count, step):
    return [(i, (i + step) % count) for i in range(count)]


def high_digit(step):
    return [(i, (i // 4 + step) % 4 * 4 + i % 4) for i in range(16)]


def low_digit(step):
    return [(i, i ^ step) for i in range(16)]


def far_pairs():
    return [(i, (i + 1) % 16 if i % 2 else (i - 1) % 16) for i in range(16)]


def body(
    features,
    fractions,
    occupied,
    wave_index,
    radial_weight,
    ewald_mix,
    msg_weight,
    ewald_weight,
    out_weight,
):
    gx, gy, gz = (lax.axis_index(name) for name in ("gx", "gy", "gz"))
    where = jnp.stack([gx, gy, gz, 1 - 2 * (gz % 2)]).astype(jnp.int32)

    def after(value, *others):
        return lax.optimization_barrier((value,) + others)[0]

    def send(value, axis, step):
        return lax.ppermute(value, axis, shifted(4, step))

    pay, cols, weight, own = call(
        prepare_kernel,
        "prepare",
        [((8, 136, 256), BF), ((512, 8), F32), ((8, 256), F32), ((8, 128, 8), F32)],
        [
            features.reshape(8, 128, 256),
            fractions.reshape(8, 3, 128),
            occupied.reshape(8, 1, 128),
            wave_index,
            radial_weight,
        ],
    )
    far = lax.ppermute(pay, "gz", far_pairs())
    near = lax.ppermute(pay, "gz", low_digit(1))
    t0, t1, t2, t3, bt = call(
        structure_kernel,
        "structure",
        [((256, 256), BF), ((272, 256), BF), ((256, 256), BF), ((272, 256), BF)]
        + [((1024, 1024), BF)],
        [where, pay, cols],
        [((8, 128), F32), ((1024, 256), F32)],
        1,
    )
    t1, t2, t3 = after((t1, t2, t3), near)
    g1, g2, g3 = (send(t, "gy", s) for s, t in ((1, t1), (2, t2), (3, t3)))
    own_low = own_messages(after(pay, t1), own, weight, 0)
    g1, g2, g3 = after((g1, g2, g3), own_low)
    u0, u1, u2, u3 = call(
        first_sum_kernel,
        "first_sum",
        [((64, 256), F32), ((112, 256), BF), ((64, 256), BF), ((112, 256), BF)],
        [t0, g1, g2, g3, pay],
    )
    h1, h2, h3 = (send(u, "gx", s) for s, u in ((1, u1), (2, u2), (3, u3)))
    own_high = own_messages(after(pay, u0), own, weight, 1)
    h1, h2, h3 = after((h1, h2, h3), own_high)
    sums, sent, home = call(
        second_sum_kernel,
        "second_sum",
        [((64, 256), F32), ((64, 256), BF), ((24, 128, 8), F32)],
        [u0, h1, h2, h3, g1, g3, own],
    )
    got = tuple(lax.ppermute(sent, "gz", high_digit(s)) for s in (1, 2, 3))
    side = side_messages(where, pay, near, home, weight)
    got = after(got, side, far)
    sums, sent = call(
        third_sum_kernel, "third_sum", [((64, 256), F32), ((64, 256), BF)], [sums, *got]
    )
    got = tuple(lax.ppermute(sent, "gz", low_digit(s)) for s in (1, 2, 3))
    low, high = far_side_messages(where, after(far, sent), home, weight, side)
    got = after(got, low)
    x1, x0, x3 = call(
        filter_kernel,
        "filter",
        [((832, 256), BF), ((64, 256), BF), ((832, 256), BF)],
        [where, sums, *got, ewald_mix, cols, low, high],
        (),
        1,
    )
    x2 = send(x0, "gx", 2)
    x1, x3 = send(x1, "gx", 1), send(x3, "gx", 3)
    late = after(near, x0)
    border, inside = rest_messages(where, pay, late, far, home, weight, own_low, own_high)
    x1, x2, x3 = after((x1, x2, x3), border)
    p1, p2, p3 = call(
        border_sum_kernel,
        "border_sum",
        [((512, 256), BF), ((256, 256), BF), ((512, 256), BF)],
        [border, x0, x1, x2, x3],
    )
    q1, q2, q3 = (send(p, "gy", s) for s, p in ((1, p1), (2, p2), (3, p3)))
    out = call(
        update_kernel,
        "update",
        [((8, 128, 256), BF)],
        [where, bt, p2, q1, q2, q3, inside, x1, x3, pay, own]
        + [msg_weight, ewald_weight, out_weight],
        [((1024, 256), BF)],
        1,
        12,
    )[0]
    return out.reshape(features.shape)


def solution(mesh):
    in_specs = (
        P("gx", "gy", "gz", None, None),
        P("gx", "gy", "gz", None, None),
        P("gx", "gy", "gz", None),
        P(),
        P(),
        P(),
        P(),
        P(),
        P(),
    )
    out_specs = P("gx", "gy", "gz", None, None)
    return jax.shard_map(body, mesh=mesh, in_specs=in_specs, out_specs=out_specs, check_vma=False)
```

```python
import math

import jax
import jax.numpy as jnp
from jax import lax
from jax.experimental import pallas as pl
from jax.experimental.pallas import tpu as pltpu
from jax.sharding import PartitionSpec as P

sharpness = 16.0
smearing = 0.04
screening = 4.0
strength = 24.0
BF = jnp.bfloat16
F32 = jnp.float32
LOG2E = 1.4426950408889634
REACH_SQ = sharpness * LOG2E
SCALE = math.sqrt(REACH_SQ)
FAR_AWAY = 1000.0
LEVELS = 8
LENGTHS = (8.0, 16.0, 16.0)
STEP = 1.0 / (LEVELS - 1)
POWER = 2.0 * sharpness * STEP * LOG2E / SCALE


def vmem():
    return pl.BlockSpec(memory_space=pltpu.VMEM)


def smem():
    return pl.BlockSpec(memory_space=pltpu.SMEM)


def anywhere():
    return pl.BlockSpec(memory_space=pl.ANY)


def call(kernel, name, outs, args, scratch=(), scalars=0, mega=8):
    return pl.pallas_call(
        kernel,
        in_specs=[smem()] * scalars + [vmem()] * (len(args) - scalars),
        out_specs=tuple(vmem() for _ in outs),
        out_shape=tuple(jax.ShapeDtypeStruct(shape, dtype) for shape, dtype in outs),
        scratch_shapes=[pltpu.VMEM(shape, dtype) for shape, dtype in scratch],
        compiler_params=pltpu.CompilerParams(vmem_limit_bytes=mega * 1024 * 1024),
        name=name,
    )(*args)


def prepare_kernel(
    feat_hbm,
    frac_hbm,
    occ_hbm,
    wave_hbm,
    radial_hbm,
    pay_ref,
    cols_ref,
    weight_ref,
    own_ref,
    left_ref,
    right_ref,
    frac_ref,
    occ_ref,
    wave_ref,
    radial_ref,
    feat_sem,
    frac_sem,
    occ_sem,
    wave_sem,
    radial_sem,
):
    copies = [
        pltpu.make_async_copy(frac_hbm, frac_ref, frac_sem),
        pltpu.make_async_copy(occ_hbm, occ_ref, occ_sem),
        pltpu.make_async_copy(wave_hbm, wave_ref, wave_sem),
        pltpu.make_async_copy(radial_hbm, radial_ref, radial_sem),
        pltpu.make_async_copy(feat_hbm, pay_ref.at[:, 0:128, :], feat_sem),
    ]
    for copy in copies:
        copy.start()
    for copy in copies[:4]:
        copy.wait()
    for n in range(8):
        x, y = n // 4, n % 4
        rows = [frac_ref[x, a].astype(F32)[y : y + 1] for a in range(3)]
        geom = jnp.concatenate(
            rows + [occ_ref[n].astype(F32), jnp.zeros((4, 128), F32)], axis=0
        )
        own_ref[n] = geom.T
        wide = jnp.concatenate([geom, jnp.zeros((8, 128), F32)], axis=1)
        pay_ref[n, 128:136, :] = wide.astype(BF)
        side = right_ref if x else left_ref
        side[y * 8 : (y + 1) * 8, :] = geom.astype(BF)
    waves = jnp.concatenate([wave_ref[...].astype(F32), jnp.zeros((5, 512), F32)], axis=0)
    for c in range(4):
        cols_ref[c * 128 : (c + 1) * 128, :] = waves[:, c * 128 : (c + 1) * 128].T
    level = lax.broadcasted_iota(jnp.int32, (8, 256), 0).astype(F32) * STEP
    lane = lax.broadcasted_iota(jnp.int32, (8, 256), 1)
    heads = jnp.concatenate([radial_ref[...], jnp.zeros((4, 8), F32)], axis=0).T
    radial = jnp.broadcast_to(heads[:, 3:4], (8, 256))
    for h in (2, 1, 0):
        radial = jnp.where(lane < 64 * (h + 1), heads[:, h : h + 1], radial)
    fixed = 1.0 / (REACH_SQ * REACH_SQ * math.sqrt(512.0))
    weight_ref[...] = radial * (jnp.exp(-sharpness * level * level) * fixed)
    copies[4].wait()


def prepare(*args):
    args = [pltpu.with_memory_space_constraint(arg, pltpu.HBM) for arg in args]
    outs = [
        ((8, 136, 256), BF),
        ((512, 8), F32),
        ((8, 256), F32),
        ((8, 128, 8), F32),
        ((32, 128), BF),
        ((32, 128), BF),
    ]
    return pl.pallas_call(
        prepare_kernel,
        in_specs=[anywhere()] * 5,
        out_specs=tuple(vmem() for _ in outs),
        out_shape=tuple(jax.ShapeDtypeStruct(shape, dtype) for shape, dtype in outs),
        scratch_shapes=[
            pltpu.VMEM((2, 3, 4, 128), BF),
            pltpu.VMEM((8, 1, 128), jnp.int32),
            pltpu.VMEM((3, 512), jnp.int32),
            pltpu.VMEM((4, 8), F32),
        ]
        + [pltpu.SemaphoreType.DMA] * 5,
        compiler_params=pltpu.CompilerParams(vmem_limit_bytes=4 * 1024 * 1024),
        name="prepare",
    )(*args)


SIN = [
    math.pi * (-1) ** i * math.pi ** (2 * i) / math.factorial(2 * i + 1) for i in range(7)
]
COS = [(-1) ** i * math.pi ** (2 * i) / math.factorial(2 * i) for i in range(7)]


def cos_sin(turns):
    part = turns - jnp.floor(turns + 0.5)
    sq = part * part
    sin_half = jnp.full_like(sq, SIN[-1])
    cos_half = jnp.full_like(sq, COS[-1])
    for i in range(len(SIN) - 2, -1, -1):
        sin_half = sin_half * sq + SIN[i]
        cos_half = cos_half * sq + COS[i]
    sin_half = sin_half * part
    twice = sin_half + sin_half
    return 1.0 - twice * sin_half, twice * cos_half


def structure_kernel(
    where_ref,
    pay_ref,
    cols_ref,
    left_ref,
    right_ref,
    t0,
    t1,
    t2,
    t3,
    bt_ref,
    mask_ref,
    total_ref,
):
    places = []
    starts = [where_ref[0] * 2, where_ref[1] * 4, where_ref[2]]
    for n in range(8):
        geom = pay_ref[n, 128:136, 0:128].astype(F32)
        cell = [starts[0] + n // 4, starts[1] + n % 4, starts[2]]
        places.append(
            [(cell[a].astype(F32) + geom[a : a + 1]) * (1.0 / LENGTHS[a]) for a in range(3)]
        )
        mask_ref[n : n + 1, :] = geom[3:4]
    for c in range(16):
        waves = cols_ref[c * 32 : (c + 1) * 32, :]
        wave = [jnp.broadcast_to(waves[:, a : a + 1], (32, 128)) for a in range(3)]
        for n in range(8):
            turns = None
            for a in range(3):
                term = wave[a] * places[n][a]
                turns = term if turns is None else turns + term
            cos, sin = cos_sin(turns)
            mask = mask_ref[n : n + 1, :]
            bt_ref[c * 64 : c * 64 + 32, n * 128 : (n + 1) * 128] = (cos * mask).astype(BF)
            bt_ref[c * 64 + 32 : c * 64 + 64, n * 128 : (n + 1) * 128] = (sin * mask).astype(BF)
    feat = jnp.concatenate([pay_ref[n, 0:128, :] for n in range(8)], axis=0)
    total_ref[...] = jnp.dot(bt_ref[...], feat, preferred_element_type=F32)
    for s, out in enumerate((t0, t1, t2, t3)):
        for r in range(4):
            start = ((where_ref[1] + s) % 4) * 256 + ((where_ref[4] + r) % 4) * 64
            rows = total_ref[pl.ds(pl.multiple_of(start, 64), 64), :]
            out[r * 64 : (r + 1) * 64, :] = rows.astype(BF)
    for out, y in ((t1, 3), (t3, 0)):
        out[256:264, :] = jnp.zeros((8, 256), BF)
        out[280:288, :] = jnp.zeros((8, 256), BF)
        out[256:264, 0:128] = left_ref[y * 8 : (y + 1) * 8, :]
        out[264:272, :] = pay_ref[y, 128:136, :]
        out[272:280, :] = pay_ref[4 + y, 128:136, :]
        out[280:288, 0:128] = right_ref[y * 8 : (y + 1) * 8, :]


def first_sum_kernel(
    t0, g1, g2, g3, own_ref, left_ref, right_ref, u0, u1, u2, u3, home_ref
):
    for r, out in enumerate((u0, u1, u2, u3)):
        rows = slice(r * 64, (r + 1) * 64)
        total = t0[rows, :].astype(F32) + g1[rows, :].astype(F32)
        total = total + (g2[rows, :].astype(F32) + g3[rows, :].astype(F32))
        out[...] = total.astype(out.dtype)
    for x in range(4):
        for y, got in ((0, g1), (5, g3)):
            home_ref[x * 6 + y] = got[256 + x * 8 : 264 + x * 8, 0:128].astype(F32).T
    for y in range(4):
        rows = slice(y * 8, (y + 1) * 8)
        home_ref[y + 1] = left_ref[rows, :].astype(F32).T
        home_ref[18 + y + 1] = right_ref[rows, :].astype(F32).T
        for x in range(2):
            home_ref[(x + 1) * 6 + y + 1] = own_ref[x * 4 + y]


def more_sum_kernel(v, a, b, c, sum_ref, sent_ref):
    total = v[...] + a[...].astype(F32) + b[...].astype(F32) + c[...].astype(F32)
    sum_ref[...] = total
    sent_ref[...] = total.astype(BF)


def filter_kernel(where_ref, w, a, b, c, mix_ref, cols_ref, out_ref):
    total = w[...] + a[...].astype(F32) + b[...].astype(F32) + c[...].astype(F32)
    mixed = jnp.dot(
        total, mix_ref[...], precision=lax.Precision.HIGHEST, preferred_element_type=F32
    )
    start = pl.multiple_of((where_ref[1] * 4 + where_ref[4]) * 32, 32)
    waves = cols_ref[pl.ds(start, 32), :]
    wave_sq = None
    for a in range(3):
        part = 2.0 * math.pi * waves[:, a : a + 1] / LENGTHS[a]
        wave_sq = part * part if wave_sq is None else wave_sq + part * part
    damping = strength * jnp.exp(-0.5 * smearing * wave_sq) / (wave_sq + screening)
    damping = damping * (1.0 / math.sqrt(262144 * 512))
    for half in range(2):
        rows = slice(half * 32, (half + 1) * 32)
        out_ref[rows, :] = (mixed[rows] * damping).astype(BF)


def border_sum_kernel(yb, x1, x3, p1, p3):
    for out, hy, side in ((p3, 0, 0), (p1, 5, 2)):
        for x, got in enumerate((x1, x3)):
            total = yb[side + x] + got[hy * 128 : (hy + 1) * 128, :].astype(F32)
            out[x * 128 : (x + 1) * 128, :] = total.astype(BF)


def bumps(home, row, eye):
    dist_sq = None
    for a in range(3):
        gap = row[a] - home[a]
        dist_sq = gap * gap if dist_sq is None else dist_sq + gap * gap
    dist_sq = jnp.minimum(dist_sq, REACH_SQ)
    if eye is not None:
        dist_sq = jnp.where(eye, REACH_SQ, dist_sq)
    rise = REACH_SQ - dist_sq
    distance = dist_sq * lax.rsqrt(jnp.maximum(dist_sq, 1e-30))
    ratio = jnp.exp2(POWER * distance)
    square = ratio * ratio
    value = rise * rise * jnp.exp2(-dist_sq)
    values = [value, value * ratio]
    for b in range(2, LEVELS):
        values.append(values[b - 2] * square)
    return values


ROWS = 16
INSIDE = [(x, y) for x in (1, 2) for y in range(1, 5)]
BORDER_X = [(x, y) for x in (0, 3) for y in range(6)]
BORDER_Y = [(x, y) for y in (0, 5) for x in (1, 2)]


def pair_sums(jobs, pay_refs, lifts, home_refs, weight_ref, y_refs, fw_refs):
    groups = []
    count = 0
    for plane, homes, accumulate in jobs:
        for source in range(8):
            sx, sy = source // 4, source % 4
            near = [
                i for i, (hx, hy) in enumerate(homes) if 0 <= hx - sx <= 2 and 0 <= hy - sy <= 2
            ]
            size = len(near) if len(near) <= 4 else (len(near) + 1) // 2
            for k in range(0, len(near), max(size, 1)):
                groups.append((plane, source, homes, near[k : k + size], accumulate, count))
            count += bool(near)

    rows_of = {}

    def fill(index):
        plane, source, homes, near, _, slot = groups[index]
        sx, sy = source // 4, source % 4
        y_ref, fw_ref = y_refs[index % 2], fw_refs[slot % 2]
        if index == 0 or groups[index - 1][5] != slot:
            feat = pay_refs[plane][source, 0:128, :].astype(F32)
            for b in range(LEVELS):
                fw_ref[b * 128 : (b + 1) * 128, :] = (feat * weight_ref[b : b + 1, :]).astype(BF)
            geom = pay_refs[plane][source, 128:136, 0:128].astype(F32)
            hide = (1.0 - geom[3:4]) * FAR_AWAY
            row = [geom[0:1] * SCALE + hide, geom[1:2] * SCALE, geom[2:3] * SCALE + lifts[plane]]
            rows_of[slot] = row
        row = rows_of[slot]
        for k, i in enumerate(near):
            hx, hy = homes[i]
            jx, jy = hx - sx, hy - sy
            moved = [row[0] + (1 - jx) * SCALE, row[1] + (1 - jy) * SCALE, row[2]]
            for r in range(0, 128, ROWS):
                cols = home_refs(hx, hy, r) * SCALE
                home = [cols[:, a : a + 1] for a in range(3)]
                eye = None
                if plane == 0 and jx == 1 and jy == 1:
                    eye = lax.broadcasted_iota(jnp.int32, (ROWS, 128), 0) + r == (
                        lax.broadcasted_iota(jnp.int32, (ROWS, 128), 1)
                    )
                at = slice(k * 128 + r, k * 128 + r + ROWS)
                for b, value in enumerate(bumps(home, moved, eye)):
                    y_ref[at, b * 128 : (b + 1) * 128] = value.astype(BF)

    def multiply(index):
        _, _, _, near, _, slot = groups[index]
        return jnp.dot(
            y_refs[index % 2][0 : len(near) * 128, :],
            fw_refs[slot % 2][...],
            preferred_element_type=F32,
        )

    def gather(index, out):
        _, _, _, near, accumulate, _ = groups[index]
        for k, i in enumerate(near):
            accumulate(i, out[k * 128 : (k + 1) * 128])

    fill(0)
    for index in range(1, len(groups)):
        out = multiply(index - 1)
        fill(index)
        gather(index - 1, out)
    gather(len(groups) - 1, multiply(len(groups) - 1))


def adder(acc_ref, start):
    seen = set()

    def accumulate(i, part):
        if i in seen:
            acc_ref[i] = acc_ref[i] + part
        else:
            seen.add(i)
            acc_ref[i] = part if start is None else start(i) + part

    return accumulate


PAIR_SCRATCH = [((512, 1024), BF)] * 2 + [((1024, 256), BF)] * 2


def own_messages(pay, own, weight):
    def kernel(pay_ref, own_ref, weight_ref, out_ref, ya, yb, fa, fb):
        def home(hx, hy, r):
            return own_ref[(hx - 1) * 4 + hy - 1, r : r + ROWS, :]

        jobs = [(0, INSIDE, adder(out_ref, None))]
        pair_sums(jobs, [pay_ref], [0.0], home, weight_ref, (ya, yb), (fa, fb))

    outs = [((8, 128, 256), F32)]
    return call(kernel, "pair_own", outs, [pay, own, weight], PAIR_SCRATCH)[0]


def inside_messages(where, feat, home, weight, old, plane):
    def kernel(where_ref, feat_ref, home_ref, weight_ref, old_ref, out_ref, *scratch):
        lift = where_ref[3].astype(F32) * SCALE
        pair_sums(
            [(plane, INSIDE, adder(out_ref, lambda i: old_ref[i]))],
            [None, feat_ref, feat_ref],
            [0.0, lift, -lift],
            lambda hx, hy, r: home_ref[hx * 6 + hy, r : r + ROWS, :],
            weight_ref,
            scratch[:2],
            scratch[2:],
        )

    outs = [((8, 128, 256), F32)]
    args = [where, feat, home, weight, old]
    return call(kernel, "pair_inside", outs, args, PAIR_SCRATCH, 1)[0]


def border_messages(where, pay, near, far, home, weight):
    def kernel(where_ref, pay_ref, near_ref, far_ref, home_ref, weight_ref, out_ref, *scratch):
        lift = where_ref[3].astype(F32) * SCALE
        add = adder(out_ref, None)
        pair_sums(
            [(plane, BORDER_Y, add) for plane in range(3)],
            [pay_ref, near_ref, far_ref],
            [0.0, lift, -lift],
            lambda hx, hy, r: home_ref[hx * 6 + hy, r : r + ROWS, :],
            weight_ref,
            scratch[:2],
            scratch[2:],
        )

    outs = [((4, 128, 256), F32)]
    args = [where, pay, near, far, home, weight]
    return call(kernel, "pair_border", outs, args, PAIR_SCRATCH, 1)[0]


def side_messages(where, pay, near, home, weight):
    def kernel(where_ref, pay_ref, near_ref, home_ref, weight_ref, out_ref, ya, yb, fa, fb):
        lift = where_ref[3].astype(F32) * SCALE
        add = adder(out_ref, None)
        pair_sums(
            [(0, BORDER_X, add), (1, BORDER_X, add)],
            [pay_ref, near_ref],
            [0.0, lift],
            lambda hx, hy, r: home_ref[hx * 6 + hy, r : r + ROWS, :],
            weight_ref,
            (ya, yb),
            (fa, fb),
        )

    outs = [((12, 128, 256), F32)]
    return call(kernel, "pair_side", outs, [where, pay, near, home, weight], PAIR_SCRATCH, 1)[0]


def far_side_messages(where, far, home, weight, side):
    def kernel(where_ref, far_ref, home_ref, weight_ref, side_ref, low, high, ya, yb, fa, fb, acc):
        lift = -where_ref[3].astype(F32) * SCALE
        pair_sums(
            [(1, BORDER_X, adder(acc, lambda i: side_ref[i]))],
            [None, far_ref],
            [0.0, lift],
            lambda hx, hy, r: home_ref[hx * 6 + hy, r : r + ROWS, :],
            weight_ref,
            (ya, yb),
            (fa, fb),
        )
        for i in range(6):
            low[i * 128 : (i + 1) * 128, :] = acc[i].astype(BF)
            high[i * 128 : (i + 1) * 128, :] = acc[6 + i].astype(BF)

    outs = [((768, 256), BF)] * 2
    scratch = PAIR_SCRATCH + [((12, 128, 256), F32)]
    return call(kernel, "pair_far_side", outs, [where, far, home, weight, side], scratch, 1)


def ewald_kernel(where_ref, bt_ref, f0, f1, f2, f3, ew, out_ref, filt):
    for s, f in enumerate((f0, f1, f2, f3)):
        for r in range(4):
            start = ((where_ref[1] - s) % 4) * 256 + ((where_ref[4] - r) % 4) * 64
            rows = f[r * 64 : (r + 1) * 64, :]
            filt[pl.ds(pl.multiple_of(start, 64), 64), :] = rows
    flipped = lax.dot_general(
        filt[...], bt_ref[...], (((0,), (0,)), ((), ())), preferred_element_type=F32
    )
    out_ref[...] = lax.dot_general(
        flipped.astype(BF), ew[...], (((0,), (0,)), ((), ())), preferred_element_type=F32
    )


def update_kernel(joined, q1, q3, in_ref, x1, x3, pay_ref, own_ref, mw, ow, out_ref):
    for x, got in enumerate((x1, x3)):
        cells = []
        for y in range(4):
            total = in_ref[x * 4 + y] + got[(y + 1) * 128 : (y + 2) * 128, :].astype(F32)
            if y == 0:
                total = total + q1[x * 128 : (x + 1) * 128, :].astype(F32)
            if y == 3:
                total = total + q3[x * 128 : (x + 1) * 128, :].astype(F32)
            cells.append(total.astype(BF))
        messages = jnp.concatenate(cells, axis=0)
        part = joined[x * 512 : (x + 1) * 512, :]
        part = part + jnp.dot(messages, mw[...], preferred_element_type=F32)
        hidden = (part / (1.0 + jnp.exp(-part))).astype(BF)
        change = jnp.dot(hidden, ow[...], preferred_element_type=F32)
        for y in range(4):
            mask = own_ref[x * 4 + y, :, 3:4]
            feat = pay_ref[x * 4 + y, 0:128, :].astype(F32)
            out_ref[x * 4 + y] = ((feat + change[y * 128 : (y + 1) * 128]) * mask).astype(BF)


def shifted(count, step):
    return [(i, (i + step) % count) for i in range(count)]


def high_digit(step):
    return [(i, (i // 4 + step) % 4 * 4 + i % 4) for i in range(16)]


def low_digit(step):
    return [(i, i ^ step) for i in range(16)]


def far_pairs():
    return [(i, (i + 1) % 16 if i % 2 else (i - 1) % 16) for i in range(16)]


def body(
    features,
    fractions,
    occupied,
    wave_index,
    radial_weight,
    ewald_mix,
    msg_weight,
    ewald_weight,
    out_weight,
):
    gx, gy, gz = (lax.axis_index(name) for name in ("gx", "gy", "gz"))
    where = jnp.stack([gx, gy, gz, 1 - 2 * (gz % 2), gz // 4]).astype(jnp.int32)

    def after(value, *others):
        return lax.optimization_barrier((value,) + others)[0]

    def send(value, axis, step):
        return lax.ppermute(value, axis, shifted(4, step))

    def send_high(value, step):
        return lax.ppermute(value, "gz", high_digit(step))

    def send_low(value, step):
        return lax.ppermute(value, "gz", low_digit(step))

    small = [((64, 256), F32), ((64, 256), BF)]
    pay, cols, weight, own, low_geom, high_geom = prepare(
        features.reshape(8, 128, 256),
        fractions.transpose(0, 2, 3, 1, 4).reshape(2, 3, 4, 128),
        occupied.reshape(8, 1, 128),
        wave_index,
        radial_weight.T,
    )
    left, right = send(high_geom, "gx", 1), send(low_geom, "gx", 3)
    sent_pay = after(pay, left, right)
    far = lax.ppermute(sent_pay, "gz", far_pairs())
    near = send_low(sent_pay, 1)
    t0, t1, t2, t3, bt = call(
        structure_kernel,
        "structure",
        [((256, 256), BF), ((288, 256), BF), ((256, 256), BF), ((288, 256), BF)]
        + [((1024, 1024), BF)],
        [where, pay, cols, left, right],
        [((8, 128), F32), ((1024, 256), F32)],
        1,
    )
    t1, t2, t3 = after((t1, t2, t3), near)
    got = tuple(send(t, "gy", s) for s, t in ((1, t1), (2, t2), (3, t3)))
    inside = own_messages(after(pay, t1), own, weight)
    got = after(got, inside)
    u0, u1, u2, u3, home = call(
        first_sum_kernel,
        "first_sum",
        [((64, 256), F32)] + [((64, 256), BF)] * 3 + [((24, 128, 8), F32)],
        [t0, *got, own, left, right],
    )
    got = tuple(send_high(u, s) for s, u in ((1, u1), (2, u2), (3, u3)))
    side = side_messages(where, pay, near, home, weight)
    got = after(got, side, far)
    sums, sent = call(more_sum_kernel, "second_sum", small, [u0, *got])
    got = tuple(send(sent, "gx", s) for s in (1, 2, 3))
    low, high = far_side_messages(where, after(far, sent), home, weight, side)
    got = after(got, low)
    sums, sent = call(more_sum_kernel, "third_sum", small, [sums, *got])
    got = tuple(send_low(sent, s) for s in (1, 2, 3))
    inside = inside_messages(where, after(near, sent), home, weight, inside, 1)
    got = after(got, inside)
    low, high = after((low, high), *got)
    x1, x3 = send(high, "gx", 1), send(low, "gx", 3)
    rows = call(
        filter_kernel,
        "filter",
        [((64, 256), BF)],
        [where, sums, *got, ewald_mix, cols],
        (),
        1,
    )[0]
    got = tuple(send_high(rows, s) for s in (1, 2, 3))
    inside = inside_messages(where, after(far, rows), home, weight, inside, 2)
    got = after(got, inside)
    rows = jnp.concatenate([rows, *got], axis=0)
    got = tuple(send(rows, "gy", s) for s in (1, 2, 3))
    border = border_messages(where, pay, near, after(far, rows), home, weight)
    got = after(got, border)
    joined = call(
        ewald_kernel,
        "ewald",
        [((1024, 256), F32)],
        [where, bt, rows, *got, ewald_weight],
        [((1024, 256), BF)],
        1,
    )[0]
    x1, x3 = after((x1, x3), border)
    p1, p3 = call(border_sum_kernel, "border_sum", [((256, 256), BF)] * 2, [border, x1, x3])
    q1, q3 = send(p1, "gy", 1), send(p3, "gy", 3)
    q1, q3 = after((q1, q3), joined)
    out = call(
        update_kernel,
        "update",
        [((8, 128, 256), BF)],
        [joined, q1, q3, inside, x1, x3, pay, own, msg_weight, out_weight],
        (),
        0,
        12,
    )[0]
    return out.reshape(features.shape)


def solution(mesh):
    in_specs = (
        P("gx", "gy", "gz", None, None),
        P("gx", "gy", "gz", None, None),
        P("gx", "gy", "gz", None),
        P(),
        P(),
        P(),
        P(),
        P(),
        P(),
    )
    out_specs = P("gx", "gy", "gz", None, None)
    return jax.shard_map(body, mesh=mesh, in_specs=in_specs, out_specs=out_specs, check_vma=False)
```

```python
import math

import jax
import jax.numpy as jnp
from jax import lax
from jax.experimental import pallas as pl
from jax.experimental.pallas import tpu as pltpu
from jax.sharding import PartitionSpec as P

sharpness = 16.0
smearing = 0.04
screening = 4.0
strength = 24.0
BF = jnp.bfloat16
F32 = jnp.float32
LOG2E = 1.4426950408889634
REACH_SQ = sharpness * LOG2E
SCALE = math.sqrt(REACH_SQ)
FAR_AWAY = 1000.0
LEVELS = 8
LENGTHS = (8.0, 16.0, 16.0)
STEP = 1.0 / (LEVELS - 1)
POWER = 2.0 * sharpness * STEP * LOG2E / SCALE


def vmem():
    return pl.BlockSpec(memory_space=pltpu.VMEM)


def smem():
    return pl.BlockSpec(memory_space=pltpu.SMEM)


def anywhere():
    return pl.BlockSpec(memory_space=pl.ANY)


def call(kernel, name, outs, args, scratch=(), scalars=0, mega=8):
    return pl.pallas_call(
        kernel,
        in_specs=[smem()] * scalars + [vmem()] * (len(args) - scalars),
        out_specs=tuple(vmem() for _ in outs),
        out_shape=tuple(jax.ShapeDtypeStruct(shape, dtype) for shape, dtype in outs),
        scratch_shapes=[pltpu.VMEM(shape, dtype) for shape, dtype in scratch],
        compiler_params=pltpu.CompilerParams(vmem_limit_bytes=mega * 1024 * 1024),
        name=name,
    )(*args)


def prepare_kernel(
    feat_hbm,
    frac_hbm,
    occ_hbm,
    wave_hbm,
    radial_hbm,
    pay_ref,
    cols_ref,
    weight_ref,
    own_ref,
    left_ref,
    right_ref,
    frac_ref,
    occ_ref,
    wave_ref,
    radial_ref,
    feat_sem,
    frac_sem,
    occ_sem,
    wave_sem,
    radial_sem,
):
    copies = [
        pltpu.make_async_copy(frac_hbm, frac_ref, frac_sem),
        pltpu.make_async_copy(occ_hbm, occ_ref, occ_sem),
        pltpu.make_async_copy(wave_hbm, wave_ref, wave_sem),
        pltpu.make_async_copy(radial_hbm, radial_ref, radial_sem),
        pltpu.make_async_copy(feat_hbm, pay_ref.at[:, 0:128, :], feat_sem),
    ]
    for copy in copies:
        copy.start()
    for copy in copies[:4]:
        copy.wait()
    for n in range(8):
        x, y = n // 4, n % 4
        rows = [frac_ref[x, a].astype(F32)[y : y + 1] for a in range(3)]
        geom = jnp.concatenate(
            rows + [occ_ref[n].astype(F32), jnp.zeros((4, 128), F32)], axis=0
        )
        own_ref[n] = geom.T
        wide = jnp.concatenate([geom, jnp.zeros((8, 128), F32)], axis=1)
        pay_ref[n, 128:136, :] = wide.astype(BF)
        side = right_ref if x else left_ref
        side[y * 8 : (y + 1) * 8, :] = geom.astype(BF)
    waves = jnp.concatenate([wave_ref[...].astype(F32), jnp.zeros((5, 512), F32)], axis=0)
    for c in range(4):
        cols_ref[c * 128 : (c + 1) * 128, :] = waves[:, c * 128 : (c + 1) * 128].T
    level = lax.broadcasted_iota(jnp.int32, (8, 256), 0).astype(F32) * STEP
    lane = lax.broadcasted_iota(jnp.int32, (8, 256), 1)
    heads = jnp.concatenate([radial_ref[...], jnp.zeros((4, 8), F32)], axis=0).T
    radial = jnp.broadcast_to(heads[:, 3:4], (8, 256))
    for h in (2, 1, 0):
        radial = jnp.where(lane < 64 * (h + 1), heads[:, h : h + 1], radial)
    fixed = 1.0 / (REACH_SQ * REACH_SQ * math.sqrt(512.0))
    weight_ref[...] = radial * (jnp.exp(-sharpness * level * level) * fixed)
    copies[4].wait()


def prepare(*args):
    args = [pltpu.with_memory_space_constraint(arg, pltpu.HBM) for arg in args]
    outs = [
        ((8, 136, 256), BF),
        ((512, 8), F32),
        ((8, 256), F32),
        ((8, 128, 8), F32),
        ((32, 128), BF),
        ((32, 128), BF),
    ]
    return pl.pallas_call(
        prepare_kernel,
        in_specs=[anywhere()] * 5,
        out_specs=tuple(vmem() for _ in outs),
        out_shape=tuple(jax.ShapeDtypeStruct(shape, dtype) for shape, dtype in outs),
        scratch_shapes=[
            pltpu.VMEM((2, 3, 4, 128), BF),
            pltpu.VMEM((8, 1, 128), jnp.int32),
            pltpu.VMEM((3, 512), jnp.int32),
            pltpu.VMEM((4, 8), F32),
        ]
        + [pltpu.SemaphoreType.DMA] * 5,
        compiler_params=pltpu.CompilerParams(vmem_limit_bytes=4 * 1024 * 1024),
        name="prepare",
    )(*args)


SIN = [
    math.pi * (-1) ** i * math.pi ** (2 * i) / math.factorial(2 * i + 1) for i in range(7)
]
COS = [(-1) ** i * math.pi ** (2 * i) / math.factorial(2 * i) for i in range(7)]


def cos_sin(turns):
    part = turns - jnp.floor(turns + 0.5)
    sq = part * part
    sin_half = jnp.full_like(sq, SIN[-1])
    cos_half = jnp.full_like(sq, COS[-1])
    for i in range(len(SIN) - 2, -1, -1):
        sin_half = sin_half * sq + SIN[i]
        cos_half = cos_half * sq + COS[i]
    sin_half = sin_half * part
    twice = sin_half + sin_half
    return 1.0 - twice * sin_half, twice * cos_half


def structure_kernel(
    where_ref,
    pay_ref,
    cols_ref,
    left_ref,
    right_ref,
    t0,
    t1,
    t2,
    t3,
    bt_ref,
    mask_ref,
    total_ref,
):
    places = []
    starts = [where_ref[0] * 2, where_ref[1] * 4, where_ref[2]]
    for n in range(8):
        geom = pay_ref[n, 128:136, 0:128].astype(F32)
        cell = [starts[0] + n // 4, starts[1] + n % 4, starts[2]]
        places.append(
            [(cell[a].astype(F32) + geom[a : a + 1]) * (1.0 / LENGTHS[a]) for a in range(3)]
        )
        mask_ref[n : n + 1, :] = geom[3:4]
    for c in range(16):
        waves = cols_ref[c * 32 : (c + 1) * 32, :]
        wave = [jnp.broadcast_to(waves[:, a : a + 1], (32, 128)) for a in range(3)]
        for n in range(8):
            turns = None
            for a in range(3):
                term = wave[a] * places[n][a]
                turns = term if turns is None else turns + term
            cos, sin = cos_sin(turns)
            mask = mask_ref[n : n + 1, :]
            bt_ref[c * 64 : c * 64 + 32, n * 128 : (n + 1) * 128] = (cos * mask).astype(BF)
            bt_ref[c * 64 + 32 : c * 64 + 64, n * 128 : (n + 1) * 128] = (sin * mask).astype(BF)
    feat = jnp.concatenate([pay_ref[n, 0:128, :] for n in range(8)], axis=0)
    total_ref[...] = jnp.dot(bt_ref[...], feat, preferred_element_type=F32)
    for s, out in enumerate((t0, t1, t2, t3)):
        for r in range(4):
            start = ((where_ref[1] + s) % 4) * 256 + ((where_ref[4] + r) % 4) * 64
            rows = total_ref[pl.ds(pl.multiple_of(start, 64), 64), :]
            out[r * 64 : (r + 1) * 64, :] = rows.astype(BF)
    for out, y in ((t1, 3), (t3, 0)):
        out[256:264, :] = jnp.zeros((8, 256), BF)
        out[280:288, :] = jnp.zeros((8, 256), BF)
        out[256:264, 0:128] = left_ref[y * 8 : (y + 1) * 8, :]
        out[264:272, :] = pay_ref[y, 128:136, :]
        out[272:280, :] = pay_ref[4 + y, 128:136, :]
        out[280:288, 0:128] = right_ref[y * 8 : (y + 1) * 8, :]


def first_sum_kernel(
    t0, g1, g2, g3, own_ref, left_ref, right_ref, u0, u1, u2, u3, home_ref
):
    for r, out in enumerate((u0, u1, u2, u3)):
        rows = slice(r * 64, (r + 1) * 64)
        total = t0[rows, :].astype(F32) + g1[rows, :].astype(F32)
        total = total + (g2[rows, :].astype(F32) + g3[rows, :].astype(F32))
        out[...] = total.astype(out.dtype)
    for x in range(4):
        for y, got in ((0, g1), (5, g3)):
            home_ref[x * 6 + y] = got[256 + x * 8 : 264 + x * 8, 0:128].astype(F32).T
    for y in range(4):
        rows = slice(y * 8, (y + 1) * 8)
        home_ref[y + 1] = left_ref[rows, :].astype(F32).T
        home_ref[18 + y + 1] = right_ref[rows, :].astype(F32).T
        for x in range(2):
            home_ref[(x + 1) * 6 + y + 1] = own_ref[x * 4 + y]


def more_sum_kernel(first, *refs):
    total = first[...]
    for part in refs[:-2]:
        total = total + part[...].astype(F32)
    refs[-2][...] = total
    refs[-1][...] = total.astype(BF)


def filter_kernel(where_ref, w, a, mix_ref, cols_ref, out_ref):
    total = w[...] + a[...].astype(F32)
    mixed = jnp.dot(
        total, mix_ref[...], precision=lax.Precision.HIGHEST, preferred_element_type=F32
    )
    start = pl.multiple_of((where_ref[1] * 4 + where_ref[4]) * 32, 32)
    waves = cols_ref[pl.ds(start, 32), :]
    wave_sq = None
    for a in range(3):
        part = 2.0 * math.pi * waves[:, a : a + 1] / LENGTHS[a]
        wave_sq = part * part if wave_sq is None else wave_sq + part * part
    damping = strength * jnp.exp(-0.5 * smearing * wave_sq) / (wave_sq + screening)
    damping = damping * (1.0 / math.sqrt(262144 * 512))
    for half in range(2):
        rows = slice(half * 32, (half + 1) * 32)
        out_ref[rows, :] = (mixed[rows] * damping).astype(BF)


def border_sum_kernel(yb, x1, x3, p1, p3):
    for out, hy, side in ((p3, 0, 0), (p1, 5, 2)):
        for x, got in enumerate((x1, x3)):
            total = yb[side + x] + got[hy * 128 : (hy + 1) * 128, :].astype(F32)
            out[x * 128 : (x + 1) * 128, :] = total.astype(BF)


def bumps(home, row, eye):
    dist_sq = None
    for a in range(3):
        gap = row[a] - home[a]
        dist_sq = gap * gap if dist_sq is None else dist_sq + gap * gap
    dist_sq = jnp.minimum(dist_sq, REACH_SQ)
    if eye is not None:
        dist_sq = jnp.where(eye, REACH_SQ, dist_sq)
    rise = REACH_SQ - dist_sq
    distance = dist_sq * lax.rsqrt(jnp.maximum(dist_sq, 1e-30))
    ratio = jnp.exp2(POWER * distance)
    square = ratio * ratio
    value = rise * rise * jnp.exp2(-dist_sq)
    values = [value, value * ratio]
    for b in range(2, LEVELS):
        values.append(values[b - 2] * square)
    return values


ROWS = 16
INSIDE = [(x, y) for x in (1, 2) for y in range(1, 5)]
BORDER_X = [(x, y) for x in (0, 3) for y in range(6)]
BORDER_Y = [(x, y) for y in (0, 5) for x in (1, 2)]


def pair_sums(jobs, pay_refs, lifts, home_refs, weight_ref, y_refs, fw_refs):
    groups = []
    count = 0
    for plane, homes, accumulate in jobs:
        for source in range(8):
            sx, sy = source // 4, source % 4
            near = [
                i for i, (hx, hy) in enumerate(homes) if 0 <= hx - sx <= 2 and 0 <= hy - sy <= 2
            ]
            size = len(near) if len(near) <= 4 else (len(near) + 1) // 2
            for k in range(0, len(near), max(size, 1)):
                groups.append((plane, source, homes, near[k : k + size], accumulate, count))
            count += bool(near)

    rows_of = {}

    def fill(index):
        plane, source, homes, near, _, slot = groups[index]
        sx, sy = source // 4, source % 4
        y_ref, fw_ref = y_refs[index % 2], fw_refs[slot % 2]
        if index == 0 or groups[index - 1][5] != slot:
            feat = pay_refs[plane][source, 0:128, :].astype(F32)
            for b in range(LEVELS):
                fw_ref[b * 128 : (b + 1) * 128, :] = (feat * weight_ref[b : b + 1, :]).astype(BF)
            geom = pay_refs[plane][source, 128:136, 0:128].astype(F32)
            hide = (1.0 - geom[3:4]) * FAR_AWAY
            row = [geom[0:1] * SCALE + hide, geom[1:2] * SCALE, geom[2:3] * SCALE + lifts[plane]]
            rows_of[slot] = row
        row = rows_of[slot]
        for k, i in enumerate(near):
            hx, hy = homes[i]
            jx, jy = hx - sx, hy - sy
            moved = [row[0] + (1 - jx) * SCALE, row[1] + (1 - jy) * SCALE, row[2]]
            for r in range(0, 128, ROWS):
                cols = home_refs(hx, hy, r) * SCALE
                home = [cols[:, a : a + 1] for a in range(3)]
                eye = None
                if plane == 0 and jx == 1 and jy == 1:
                    eye = lax.broadcasted_iota(jnp.int32, (ROWS, 128), 0) + r == (
                        lax.broadcasted_iota(jnp.int32, (ROWS, 128), 1)
                    )
                at = slice(k * 128 + r, k * 128 + r + ROWS)
                for b, value in enumerate(bumps(home, moved, eye)):
                    y_ref[at, b * 128 : (b + 1) * 128] = value.astype(BF)

    def multiply(index):
        _, _, _, near, _, slot = groups[index]
        return jnp.dot(
            y_refs[index % 2][0 : len(near) * 128, :],
            fw_refs[slot % 2][...],
            preferred_element_type=F32,
        )

    def gather(index, out):
        _, _, _, near, accumulate, _ = groups[index]
        for k, i in enumerate(near):
            accumulate(i, out[k * 128 : (k + 1) * 128])

    fill(0)
    for index in range(1, len(groups)):
        out = multiply(index - 1)
        fill(index)
        gather(index - 1, out)
    gather(len(groups) - 1, multiply(len(groups) - 1))


def adder(acc_ref, start):
    seen = set()

    def accumulate(i, part):
        if i in seen:
            acc_ref[i] = acc_ref[i] + part
        else:
            seen.add(i)
            acc_ref[i] = part if start is None else start(i) + part

    return accumulate


PAIR_SCRATCH = [((512, 1024), BF)] * 2 + [((1024, 256), BF)] * 2


def own_messages(pay, own, weight):
    def kernel(pay_ref, own_ref, weight_ref, out_ref, ya, yb, fa, fb):
        def home(hx, hy, r):
            return own_ref[(hx - 1) * 4 + hy - 1, r : r + ROWS, :]

        jobs = [(0, INSIDE, adder(out_ref, None))]
        pair_sums(jobs, [pay_ref], [0.0], home, weight_ref, (ya, yb), (fa, fb))

    outs = [((8, 128, 256), F32)]
    return call(kernel, "pair_own", outs, [pay, own, weight], PAIR_SCRATCH)[0]


def plane_messages(where, feat, home, weight, old, homes, plane, name):
    def kernel(where_ref, feat_ref, home_ref, weight_ref, *refs):
        lift = where_ref[3].astype(F32) * SCALE
        if old is None:
            start = None
        else:
            old_ref, refs = refs[0], refs[1:]
            start = lambda i: old_ref[i]
        pair_sums(
            [(plane, homes, adder(refs[0], start))],
            [feat_ref] * 3,
            [0.0, lift, -lift],
            lambda hx, hy, r: home_ref[hx * 6 + hy, r : r + ROWS, :],
            weight_ref,
            refs[1:3],
            refs[3:5],
        )

    outs = [((len(homes), 128, 256), F32)]
    args = [where, feat, home, weight] + ([] if old is None else [old])
    return call(kernel, name, outs, args, PAIR_SCRATCH, 1)[0]


def border_messages(where, pay, near, far, home, weight):
    def kernel(where_ref, pay_ref, near_ref, far_ref, home_ref, weight_ref, out_ref, *scratch):
        lift = where_ref[3].astype(F32) * SCALE
        add = adder(out_ref, None)
        pair_sums(
            [(plane, BORDER_Y, add) for plane in range(3)],
            [pay_ref, near_ref, far_ref],
            [0.0, lift, -lift],
            lambda hx, hy, r: home_ref[hx * 6 + hy, r : r + ROWS, :],
            weight_ref,
            scratch[:2],
            scratch[2:],
        )

    outs = [((4, 128, 256), F32)]
    args = [where, pay, near, far, home, weight]
    return call(kernel, "pair_border", outs, args, PAIR_SCRATCH, 1)[0]


def far_side_messages(where, far, home, weight, side):
    def kernel(where_ref, far_ref, home_ref, weight_ref, side_ref, low, high, ya, yb, fa, fb, acc):
        lift = -where_ref[3].astype(F32) * SCALE
        pair_sums(
            [(1, BORDER_X, adder(acc, lambda i: side_ref[i]))],
            [None, far_ref],
            [0.0, lift],
            lambda hx, hy, r: home_ref[hx * 6 + hy, r : r + ROWS, :],
            weight_ref,
            (ya, yb),
            (fa, fb),
        )
        for i in range(6):
            low[i * 128 : (i + 1) * 128, :] = acc[i].astype(BF)
            high[i * 128 : (i + 1) * 128, :] = acc[6 + i].astype(BF)

    outs = [((768, 256), BF)] * 2
    scratch = PAIR_SCRATCH + [((12, 128, 256), F32)]
    return call(kernel, "pair_far_side", outs, [where, far, home, weight, side], scratch, 1)


def ewald_kernel(where_ref, bt_ref, f0, f1, f2, f3, ew, out_ref, filt):
    for s, f in enumerate((f0, f1, f2, f3)):
        for r in range(4):
            start = ((where_ref[1] - s) % 4) * 256 + ((where_ref[4] - r) % 4) * 64
            rows = f[r * 64 : (r + 1) * 64, :]
            filt[pl.ds(pl.multiple_of(start, 64), 64), :] = rows
    flipped = lax.dot_general(
        filt[...], bt_ref[...], (((0,), (0,)), ((), ())), preferred_element_type=F32
    )
    out_ref[...] = lax.dot_general(
        flipped.astype(BF), ew[...], (((0,), (0,)), ((), ())), preferred_element_type=F32
    )


def update_kernel(joined, q1, q3, in_ref, x1, x3, pay_ref, own_ref, mw, ow, out_ref):
    for x, got in enumerate((x1, x3)):
        cells = []
        for y in range(4):
            total = in_ref[x * 4 + y] + got[(y + 1) * 128 : (y + 2) * 128, :].astype(F32)
            if y == 0:
                total = total + q1[x * 128 : (x + 1) * 128, :].astype(F32)
            if y == 3:
                total = total + q3[x * 128 : (x + 1) * 128, :].astype(F32)
            cells.append(total.astype(BF))
        messages = jnp.concatenate(cells, axis=0)
        part = joined[x * 512 : (x + 1) * 512, :]
        part = part + jnp.dot(messages, mw[...], preferred_element_type=F32)
        hidden = (part / (1.0 + jnp.exp(-part))).astype(BF)
        change = jnp.dot(hidden, ow[...], preferred_element_type=F32)
        for y in range(4):
            mask = own_ref[x * 4 + y, :, 3:4]
            feat = pay_ref[x * 4 + y, 0:128, :].astype(F32)
            out_ref[x * 4 + y] = ((feat + change[y * 128 : (y + 1) * 128]) * mask).astype(BF)


def shifted(count, step):
    return [(i, (i + step) % count) for i in range(count)]


def high_digit(step):
    return [(i, (i // 4 + step) % 4 * 4 + i % 4) for i in range(16)]


def low_digit(step):
    return [(i, i ^ step) for i in range(16)]


def far_pairs():
    return [(i, (i + 1) % 16 if i % 2 else (i - 1) % 16) for i in range(16)]


def body(
    features,
    fractions,
    occupied,
    wave_index,
    radial_weight,
    ewald_mix,
    msg_weight,
    ewald_weight,
    out_weight,
):
    gx, gy, gz = (lax.axis_index(name) for name in ("gx", "gy", "gz"))
    where = jnp.stack([gx, gy, gz, 1 - 2 * (gz % 2), gz // 4]).astype(jnp.int32)

    def after(value, *others):
        return lax.optimization_barrier((value,) + others)[0]

    def send(value, axis, step):
        return lax.ppermute(value, axis, shifted(4, step))

    def send_high(value, step):
        return lax.ppermute(value, "gz", high_digit(step))

    def send_low(value, step):
        return lax.ppermute(value, "gz", low_digit(step))

    small = [((64, 256), F32), ((64, 256), BF)]
    pay, cols, weight, own, low_geom, high_geom = prepare(
        features.reshape(8, 128, 256),
        fractions.transpose(0, 2, 3, 1, 4).reshape(2, 3, 4, 128),
        occupied.reshape(8, 1, 128),
        wave_index,
        radial_weight.T,
    )
    left, right = send(high_geom, "gx", 1), send(low_geom, "gx", 3)
    sent_pay = after(pay, left, right)
    far = lax.ppermute(sent_pay, "gz", far_pairs())
    near = send_low(sent_pay, 1)
    t0, t1, t2, t3, bt = call(
        structure_kernel,
        "structure",
        [((256, 256), BF), ((288, 256), BF), ((256, 256), BF), ((288, 256), BF)]
        + [((1024, 1024), BF)],
        [where, pay, cols, left, right],
        [((8, 128), F32), ((1024, 256), F32)],
        1,
    )
    t1, t2, t3 = after((t1, t2, t3), near)
    got = tuple(send(t, "gy", s) for s, t in ((1, t1), (2, t2), (3, t3)))
    inside = own_messages(after(pay, t1), own, weight)
    got = after(got, inside)
    u0, u1, u2, u3, home = call(
        first_sum_kernel,
        "first_sum",
        [((64, 256), F32)] + [((64, 256), BF)] * 3 + [((24, 128, 8), F32)],
        [t0, *got, own, left, right],
    )
    got = tuple(send_high(u, s) for s, u in ((1, u1), (2, u2), (3, u3)))
    side = plane_messages(where, pay, home, weight, None, BORDER_X, 0, "pair_side_own")
    got = after(got, side)
    sums, sent = call(more_sum_kernel, "second_sum", small, [u0, *got])
    got = send_low(sent, 1)
    side = plane_messages(
        where, after(near, sent), home, weight, side, BORDER_X, 1, "pair_side_near"
    )
    got = after(got, side, far)
    sums, sent = call(more_sum_kernel, "third_sum", small, [sums, got])
    got = tuple(send(sent, "gx", s) for s in (1, 2, 3))
    low, high = far_side_messages(where, after(far, sent), home, weight, side)
    got = after(got, low)
    sums, sent = call(more_sum_kernel, "fourth_sum", small, [sums, *got])
    got = send_low(sent, 2)
    inside = plane_messages(
        where, after(near, sent), home, weight, inside, INSIDE, 1, "pair_inside_near"
    )
    got = after(got, inside)
    low, high = after((low, high), got)
    x1, x3 = send(high, "gx", 1), send(low, "gx", 3)
    rows = call(
        filter_kernel,
        "filter",
        [((64, 256), BF)],
        [where, sums, got, ewald_mix, cols],
        (),
        1,
    )[0]
    got = tuple(send_high(rows, s) for s in (1, 2, 3))
    inside = plane_messages(
        where, after(far, rows), home, weight, inside, INSIDE, 2, "pair_inside_far"
    )
    got = after(got, inside)
    rows = jnp.concatenate([rows, *got], axis=0)
    got = tuple(send(rows, "gy", s) for s in (1, 2, 3))
    border = border_messages(where, pay, near, after(far, rows), home, weight)
    got = after(got, border)
    joined = call(
        ewald_kernel,
        "ewald",
        [((1024, 256), F32)],
        [where, bt, rows, *got, ewald_weight],
        [((1024, 256), BF)],
        1,
    )[0]
    x1, x3 = after((x1, x3), border)
    p1, p3 = call(border_sum_kernel, "border_sum", [((256, 256), BF)] * 2, [border, x1, x3])
    q1, q3 = send(p1, "gy", 1), send(p3, "gy", 3)
    q1, q3 = after((q1, q3), joined)
    out = call(
        update_kernel,
        "update",
        [((8, 128, 256), BF)],
        [joined, q1, q3, inside, x1, x3, pay, own, msg_weight, out_weight],
        (),
        0,
        12,
    )[0]
    return out.reshape(features.shape)


def solution(mesh):
    in_specs = (
        P("gx", "gy", "gz", None, None),
        P("gx", "gy", "gz", None, None),
        P("gx", "gy", "gz", None),
        P(),
        P(),
        P(),
        P(),
        P(),
        P(),
    )
    out_specs = P("gx", "gy", "gz", None, None)
    return jax.shard_map(body, mesh=mesh, in_specs=in_specs, out_specs=out_specs, check_vma=False)
```

```python
import math

import jax
import jax.numpy as jnp
from jax import lax
from jax.experimental import pallas as pl
from jax.experimental.pallas import tpu as pltpu
from jax.sharding import PartitionSpec as P

sharpness = 16.0
smearing = 0.04
screening = 4.0
strength = 24.0
BF = jnp.bfloat16
F32 = jnp.float32
LOG2E = 1.4426950408889634
REACH_SQ = sharpness * LOG2E
SCALE = math.sqrt(REACH_SQ)
FAR_AWAY = 1000.0
LEVELS = 8
LENGTHS = (8.0, 16.0, 16.0)
STEP = 1.0 / (LEVELS - 1)
POWER = 2.0 * sharpness * STEP * LOG2E / SCALE


def vmem():
    return pl.BlockSpec(memory_space=pltpu.VMEM)


def smem():
    return pl.BlockSpec(memory_space=pltpu.SMEM)


def anywhere():
    return pl.BlockSpec(memory_space=pl.ANY)


def call(kernel, name, outs, args, scratch=(), scalars=0, mega=8):
    return pl.pallas_call(
        kernel,
        in_specs=[smem()] * scalars + [vmem()] * (len(args) - scalars),
        out_specs=tuple(vmem() for _ in outs),
        out_shape=tuple(jax.ShapeDtypeStruct(shape, dtype) for shape, dtype in outs),
        scratch_shapes=[pltpu.VMEM(shape, dtype) for shape, dtype in scratch],
        compiler_params=pltpu.CompilerParams(vmem_limit_bytes=mega * 1024 * 1024),
        name=name,
    )(*args)


def prepare_kernel(
    feat_hbm,
    frac_hbm,
    occ_hbm,
    wave_hbm,
    radial_hbm,
    pay_ref,
    cols_ref,
    weight_ref,
    own_ref,
    left_ref,
    right_ref,
    frac_ref,
    occ_ref,
    wave_ref,
    radial_ref,
    feat_sem,
    frac_sem,
    occ_sem,
    wave_sem,
    radial_sem,
):
    copies = [
        pltpu.make_async_copy(frac_hbm, frac_ref, frac_sem),
        pltpu.make_async_copy(occ_hbm, occ_ref, occ_sem),
        pltpu.make_async_copy(wave_hbm, wave_ref, wave_sem),
        pltpu.make_async_copy(radial_hbm, radial_ref, radial_sem),
        pltpu.make_async_copy(feat_hbm, pay_ref.at[:, 0:128, :], feat_sem),
    ]
    for copy in copies:
        copy.start()
    for copy in copies[:4]:
        copy.wait()
    for n in range(8):
        x, y = n // 4, n % 4
        rows = [frac_ref[x, a].astype(F32)[y : y + 1] for a in range(3)]
        geom = jnp.concatenate(
            rows + [occ_ref[n].astype(F32), jnp.zeros((4, 128), F32)], axis=0
        )
        own_ref[n] = geom.T
        wide = jnp.concatenate([geom, jnp.zeros((8, 128), F32)], axis=1)
        pay_ref[n, 128:136, :] = wide.astype(BF)
        side = right_ref if x else left_ref
        side[y * 8 : (y + 1) * 8, :] = geom.astype(BF)
    waves = jnp.concatenate([wave_ref[...].astype(F32), jnp.zeros((5, 512), F32)], axis=0)
    for c in range(4):
        cols_ref[c * 128 : (c + 1) * 128, :] = waves[:, c * 128 : (c + 1) * 128].T
    level = lax.broadcasted_iota(jnp.int32, (8, 256), 0).astype(F32) * STEP
    lane = lax.broadcasted_iota(jnp.int32, (8, 256), 1)
    heads = jnp.concatenate([radial_ref[...], jnp.zeros((4, 8), F32)], axis=0).T
    radial = jnp.broadcast_to(heads[:, 3:4], (8, 256))
    for h in (2, 1, 0):
        radial = jnp.where(lane < 64 * (h + 1), heads[:, h : h + 1], radial)
    fixed = 1.0 / (REACH_SQ * REACH_SQ * math.sqrt(512.0))
    weight_ref[...] = radial * (jnp.exp(-sharpness * level * level) * fixed)
    copies[4].wait()


def prepare(*args):
    args = [pltpu.with_memory_space_constraint(arg, pltpu.HBM) for arg in args]
    outs = [
        ((8, 136, 256), BF),
        ((512, 8), F32),
        ((8, 256), F32),
        ((8, 128, 8), F32),
        ((32, 128), BF),
        ((32, 128), BF),
    ]
    return pl.pallas_call(
        prepare_kernel,
        in_specs=[anywhere()] * 5,
        out_specs=tuple(vmem() for _ in outs),
        out_shape=tuple(jax.ShapeDtypeStruct(shape, dtype) for shape, dtype in outs),
        scratch_shapes=[
            pltpu.VMEM((2, 3, 4, 128), BF),
            pltpu.VMEM((8, 1, 128), jnp.int32),
            pltpu.VMEM((3, 512), jnp.int32),
            pltpu.VMEM((4, 8), F32),
        ]
        + [pltpu.SemaphoreType.DMA] * 5,
        compiler_params=pltpu.CompilerParams(vmem_limit_bytes=4 * 1024 * 1024),
        name="prepare",
    )(*args)


SIN = [
    math.pi * (-1) ** i * math.pi ** (2 * i) / math.factorial(2 * i + 1) for i in range(7)
]
COS = [(-1) ** i * math.pi ** (2 * i) / math.factorial(2 * i) for i in range(7)]


def cos_sin(turns):
    part = turns - jnp.floor(turns + 0.5)
    sq = part * part
    sin_half = jnp.full_like(sq, SIN[-1])
    cos_half = jnp.full_like(sq, COS[-1])
    for i in range(len(SIN) - 2, -1, -1):
        sin_half = sin_half * sq + SIN[i]
        cos_half = cos_half * sq + COS[i]
    sin_half = sin_half * part
    twice = sin_half + sin_half
    return 1.0 - twice * sin_half, twice * cos_half


def structure_kernel(
    where_ref,
    pay_ref,
    cols_ref,
    left_ref,
    right_ref,
    t0,
    t1,
    t2,
    t3,
    bt_ref,
    mask_ref,
    total_ref,
):
    places = []
    starts = [where_ref[0] * 2, where_ref[1] * 4, where_ref[2]]
    for n in range(8):
        geom = pay_ref[n, 128:136, 0:128].astype(F32)
        cell = [starts[0] + n // 4, starts[1] + n % 4, starts[2]]
        places.append(
            [(cell[a].astype(F32) + geom[a : a + 1]) * (1.0 / LENGTHS[a]) for a in range(3)]
        )
        mask_ref[n : n + 1, :] = geom[3:4]
    for c in range(16):
        waves = cols_ref[c * 32 : (c + 1) * 32, :]
        wave = [jnp.broadcast_to(waves[:, a : a + 1], (32, 128)) for a in range(3)]
        for n in range(8):
            turns = None
            for a in range(3):
                term = wave[a] * places[n][a]
                turns = term if turns is None else turns + term
            cos, sin = cos_sin(turns)
            mask = mask_ref[n : n + 1, :]
            bt_ref[c * 64 : c * 64 + 32, n * 128 : (n + 1) * 128] = (cos * mask).astype(BF)
            bt_ref[c * 64 + 32 : c * 64 + 64, n * 128 : (n + 1) * 128] = (sin * mask).astype(BF)
    feat = jnp.concatenate([pay_ref[n, 0:128, :] for n in range(8)], axis=0)
    total_ref[...] = jnp.dot(bt_ref[...], feat, preferred_element_type=F32)
    for s, out in enumerate((t0, t1, t2, t3)):
        for r in range(4):
            start = ((where_ref[1] + s) % 4) * 256 + ((where_ref[4] + r) % 4) * 64
            rows = total_ref[pl.ds(pl.multiple_of(start, 64), 64), :]
            out[r * 64 : (r + 1) * 64, :] = rows.astype(BF)
    for out, y in ((t1, 3), (t3, 0)):
        out[256:264, :] = jnp.zeros((8, 256), BF)
        out[280:288, :] = jnp.zeros((8, 256), BF)
        out[256:264, 0:128] = left_ref[y * 8 : (y + 1) * 8, :]
        out[264:272, :] = pay_ref[y, 128:136, :]
        out[272:280, :] = pay_ref[4 + y, 128:136, :]
        out[280:288, 0:128] = right_ref[y * 8 : (y + 1) * 8, :]


def first_sum_kernel(
    t0, g1, g2, g3, own_ref, left_ref, right_ref, u0, u1, u2, u3, home_ref
):
    for r, out in enumerate((u0, u1, u2, u3)):
        rows = slice(r * 64, (r + 1) * 64)
        total = t0[rows, :].astype(F32) + g1[rows, :].astype(F32)
        total = total + (g2[rows, :].astype(F32) + g3[rows, :].astype(F32))
        out[...] = total.astype(out.dtype)
    for x in range(4):
        for y, got in ((0, g1), (5, g3)):
            home_ref[x * 6 + y] = got[256 + x * 8 : 264 + x * 8, 0:128].astype(F32).T
    for y in range(4):
        rows = slice(y * 8, (y + 1) * 8)
        home_ref[y + 1] = left_ref[rows, :].astype(F32).T
        home_ref[18 + y + 1] = right_ref[rows, :].astype(F32).T
        for x in range(2):
            home_ref[(x + 1) * 6 + y + 1] = own_ref[x * 4 + y]


def more_sum_kernel(first, *refs):
    total = first[...]
    for part in refs[:-2]:
        total = total + part[...].astype(F32)
    refs[-2][...] = total
    refs[-1][...] = total.astype(BF)


def filter_kernel(where_ref, w, a, mix_ref, cols_ref, out_ref):
    total = w[...] + a[...].astype(F32)
    mixed = jnp.dot(
        total, mix_ref[...], precision=lax.Precision.HIGHEST, preferred_element_type=F32
    )
    start = pl.multiple_of((where_ref[1] * 4 + where_ref[4]) * 32, 32)
    waves = cols_ref[pl.ds(start, 32), :]
    wave_sq = None
    for a in range(3):
        part = 2.0 * math.pi * waves[:, a : a + 1] / LENGTHS[a]
        wave_sq = part * part if wave_sq is None else wave_sq + part * part
    damping = strength * jnp.exp(-0.5 * smearing * wave_sq) / (wave_sq + screening)
    damping = damping * (1.0 / math.sqrt(262144 * 512))
    for half in range(2):
        rows = slice(half * 32, (half + 1) * 32)
        out_ref[rows, :] = (mixed[rows] * damping).astype(BF)


def border_sum_kernel(yb, x1, x3, p1, p3):
    for out, hy, side in ((p3, 0, 0), (p1, 5, 2)):
        for x, got in enumerate((x1, x3)):
            total = yb[side + x] + got[hy * 128 : (hy + 1) * 128, :].astype(F32)
            out[x * 128 : (x + 1) * 128, :] = total.astype(BF)


def bumps(home, row, eye):
    dist_sq = None
    for a in range(3):
        gap = row[a] - home[a]
        dist_sq = gap * gap if dist_sq is None else dist_sq + gap * gap
    dist_sq = jnp.minimum(dist_sq, REACH_SQ)
    if eye is not None:
        dist_sq = jnp.where(eye, REACH_SQ, dist_sq)
    rise = REACH_SQ - dist_sq
    distance = dist_sq * lax.rsqrt(jnp.maximum(dist_sq, 1e-30))
    ratio = jnp.exp2(POWER * distance)
    square = ratio * ratio
    value = rise * rise * jnp.exp2(-dist_sq)
    values = [value, value * ratio]
    for b in range(2, LEVELS):
        values.append(values[b - 2] * square)
    return values


ROWS = 16
INSIDE = [(x, y) for x in (1, 2) for y in range(1, 5)]
BORDER_X = [(x, y) for x in (0, 3) for y in range(6)]
BORDER_Y = [(x, y) for y in (0, 5) for x in (1, 2)]


def pair_sums(jobs, pay_refs, lifts, home_refs, weight_ref, y_refs, fw_refs):
    groups = []
    count = 0
    for plane, homes, accumulate in jobs:
        for source in range(8):
            sx, sy = source // 4, source % 4
            near = [
                i for i, (hx, hy) in enumerate(homes) if 0 <= hx - sx <= 2 and 0 <= hy - sy <= 2
            ]
            chunks = max(-(-len(near) // 4), 1)
            size = max(-(-len(near) // chunks), 1)
            for k in range(0, len(near), size):
                groups.append((plane, source, homes, near[k : k + size], accumulate, count))
            count += bool(near)

    rows_of = {}

    def fill(index):
        plane, source, homes, near, _, slot = groups[index]
        sx, sy = source // 4, source % 4
        y_ref, fw_ref = y_refs[index % 2], fw_refs[slot % 2]
        if index == 0 or groups[index - 1][5] != slot:
            feat = pay_refs[plane][source, 0:128, :].astype(F32)
            for b in range(LEVELS):
                fw_ref[b * 128 : (b + 1) * 128, :] = (feat * weight_ref[b : b + 1, :]).astype(BF)
            geom = pay_refs[plane][source, 128:136, 0:128].astype(F32)
            hide = (1.0 - geom[3:4]) * FAR_AWAY
            row = [geom[0:1] * SCALE + hide, geom[1:2] * SCALE, geom[2:3] * SCALE + lifts[plane]]
            rows_of[slot] = row
        row = rows_of[slot]
        for k, i in enumerate(near):
            hx, hy = homes[i]
            jx, jy = hx - sx, hy - sy
            moved = [row[0] + (1 - jx) * SCALE, row[1] + (1 - jy) * SCALE, row[2]]
            for r in range(0, 128, ROWS):
                cols = home_refs(hx, hy, r) * SCALE
                home = [cols[:, a : a + 1] for a in range(3)]
                eye = None
                if plane == 0 and jx == 1 and jy == 1:
                    eye = lax.broadcasted_iota(jnp.int32, (ROWS, 128), 0) + r == (
                        lax.broadcasted_iota(jnp.int32, (ROWS, 128), 1)
                    )
                at = slice(k * 128 + r, k * 128 + r + ROWS)
                for b, value in enumerate(bumps(home, moved, eye)):
                    y_ref[at, b * 128 : (b + 1) * 128] = value.astype(BF)

    def multiply(index):
        _, _, _, near, _, slot = groups[index]
        return jnp.dot(
            y_refs[index % 2][0 : len(near) * 128, :],
            fw_refs[slot % 2][...],
            preferred_element_type=F32,
        )

    def gather(index, out):
        _, _, _, near, accumulate, _ = groups[index]
        for k, i in enumerate(near):
            accumulate(i, out[k * 128 : (k + 1) * 128])

    fill(0)
    for index in range(1, len(groups)):
        out = multiply(index - 1)
        fill(index)
        gather(index - 1, out)
    gather(len(groups) - 1, multiply(len(groups) - 1))


def adder(acc_ref, start):
    seen = set()

    def accumulate(i, part):
        if i in seen:
            acc_ref[i] = acc_ref[i] + part
        else:
            seen.add(i)
            acc_ref[i] = part if start is None else start(i) + part

    return accumulate


PAIR_SCRATCH = [((512, 1024), BF)] * 2 + [((1024, 256), BF)] * 2


def own_messages(pay, own, weight):
    def kernel(pay_ref, own_ref, weight_ref, out_ref, ya, yb, fa, fb):
        def home(hx, hy, r):
            return own_ref[(hx - 1) * 4 + hy - 1, r : r + ROWS, :]

        jobs = [(0, INSIDE, adder(out_ref, None))]
        pair_sums(jobs, [pay_ref], [0.0], home, weight_ref, (ya, yb), (fa, fb))

    outs = [((8, 128, 256), F32)]
    return call(kernel, "pair_own", outs, [pay, own, weight], PAIR_SCRATCH)[0]


def plane_messages(where, feat, home, weight, old, homes, plane, name):
    def kernel(where_ref, feat_ref, home_ref, weight_ref, *refs):
        lift = where_ref[3].astype(F32) * SCALE
        if old is None:
            start = None
        else:
            old_ref, refs = refs[0], refs[1:]
            start = lambda i: old_ref[i]
        pair_sums(
            [(plane, homes, adder(refs[0], start))],
            [feat_ref] * 3,
            [0.0, lift, -lift],
            lambda hx, hy, r: home_ref[hx * 6 + hy, r : r + ROWS, :],
            weight_ref,
            refs[1:3],
            refs[3:5],
        )

    outs = [((len(homes), 128, 256), F32)]
    args = [where, feat, home, weight] + ([] if old is None else [old])
    return call(kernel, name, outs, args, PAIR_SCRATCH, 1)[0]


def near_messages(where, feat, home, weight, old_side, old_inside):
    homes = BORDER_X + INSIDE
    count = len(BORDER_X)

    def kernel(where_ref, feat_ref, home_ref, weight_ref, a, b, side_ref, in_ref, *scratch):
        side = adder(side_ref, lambda i: a[i])
        inside = adder(in_ref, lambda i: b[i])

        def accumulate(i, part):
            if i < count:
                side(i, part)
            else:
                inside(i - count, part)

        pair_sums(
            [(1, homes, accumulate)],
            [None, feat_ref],
            [0.0, where_ref[3].astype(F32) * SCALE],
            lambda hx, hy, r: home_ref[hx * 6 + hy, r : r + ROWS, :],
            weight_ref,
            scratch[:2],
            scratch[2:],
        )

    outs = [((12, 128, 256), F32), ((8, 128, 256), F32)]
    args = [where, feat, home, weight, old_side, old_inside]
    return call(kernel, "pair_near", outs, args, PAIR_SCRATCH, 1)


def border_messages(where, pay, near, far, home, weight):
    def kernel(where_ref, pay_ref, near_ref, far_ref, home_ref, weight_ref, out_ref, *scratch):
        lift = where_ref[3].astype(F32) * SCALE
        add = adder(out_ref, None)
        pair_sums(
            [(plane, BORDER_Y, add) for plane in range(3)],
            [pay_ref, near_ref, far_ref],
            [0.0, lift, -lift],
            lambda hx, hy, r: home_ref[hx * 6 + hy, r : r + ROWS, :],
            weight_ref,
            scratch[:2],
            scratch[2:],
        )

    outs = [((4, 128, 256), F32)]
    args = [where, pay, near, far, home, weight]
    return call(kernel, "pair_border", outs, args, PAIR_SCRATCH, 1)[0]


def far_side_messages(where, far, home, weight, side):
    def kernel(where_ref, far_ref, home_ref, weight_ref, side_ref, low, high, ya, yb, fa, fb, acc):
        lift = -where_ref[3].astype(F32) * SCALE
        pair_sums(
            [(1, BORDER_X, adder(acc, lambda i: side_ref[i]))],
            [None, far_ref],
            [0.0, lift],
            lambda hx, hy, r: home_ref[hx * 6 + hy, r : r + ROWS, :],
            weight_ref,
            (ya, yb),
            (fa, fb),
        )
        for i in range(6):
            low[i * 128 : (i + 1) * 128, :] = acc[i].astype(BF)
            high[i * 128 : (i + 1) * 128, :] = acc[6 + i].astype(BF)

    outs = [((768, 256), BF)] * 2
    scratch = PAIR_SCRATCH + [((12, 128, 256), F32)]
    return call(kernel, "pair_far_side", outs, [where, far, home, weight, side], scratch, 1)


def ewald_kernel(where_ref, bt_ref, f0, f1, f2, f3, ew, out_ref, filt):
    for s, f in enumerate((f0, f1, f2, f3)):
        for r in range(4):
            start = ((where_ref[1] - s) % 4) * 256 + ((where_ref[4] - r) % 4) * 64
            rows = f[r * 64 : (r + 1) * 64, :]
            filt[pl.ds(pl.multiple_of(start, 64), 64), :] = rows
    flipped = lax.dot_general(
        filt[...], bt_ref[...], (((0,), (0,)), ((), ())), preferred_element_type=F32
    )
    out_ref[...] = lax.dot_general(
        flipped.astype(BF), ew[...], (((0,), (0,)), ((), ())), preferred_element_type=F32
    )


def update_kernel(joined, q1, q3, in_ref, x1, x3, pay_ref, own_ref, mw, ow, out_ref):
    for x, got in enumerate((x1, x3)):
        cells = []
        for y in range(4):
            total = in_ref[x * 4 + y] + got[(y + 1) * 128 : (y + 2) * 128, :].astype(F32)
            if y == 0:
                total = total + q1[x * 128 : (x + 1) * 128, :].astype(F32)
            if y == 3:
                total = total + q3[x * 128 : (x + 1) * 128, :].astype(F32)
            cells.append(total.astype(BF))
        messages = jnp.concatenate(cells, axis=0)
        part = joined[x * 512 : (x + 1) * 512, :]
        part = part + jnp.dot(messages, mw[...], preferred_element_type=F32)
        hidden = (part / (1.0 + jnp.exp(-part))).astype(BF)
        change = jnp.dot(hidden, ow[...], preferred_element_type=F32)
        for y in range(4):
            mask = own_ref[x * 4 + y, :, 3:4]
            feat = pay_ref[x * 4 + y, 0:128, :].astype(F32)
            out_ref[x * 4 + y] = ((feat + change[y * 128 : (y + 1) * 128]) * mask).astype(BF)


def shifted(count, step):
    return [(i, (i + step) % count) for i in range(count)]


def high_digit(step):
    return [(i, (i // 4 + step) % 4 * 4 + i % 4) for i in range(16)]


def low_digit(step):
    return [(i, i ^ step) for i in range(16)]


def far_pairs():
    return [(i, (i + 1) % 16 if i % 2 else (i - 1) % 16) for i in range(16)]


def body(
    features,
    fractions,
    occupied,
    wave_index,
    radial_weight,
    ewald_mix,
    msg_weight,
    ewald_weight,
    out_weight,
):
    gx, gy, gz = (lax.axis_index(name) for name in ("gx", "gy", "gz"))
    where = jnp.stack([gx, gy, gz, 1 - 2 * (gz % 2), gz // 4]).astype(jnp.int32)

    def after(value, *others):
        return lax.optimization_barrier((value,) + others)[0]

    def send(value, axis, step):
        return lax.ppermute(value, axis, shifted(4, step))

    def send_high(value, step):
        return lax.ppermute(value, "gz", high_digit(step))

    def send_low(value, step):
        return lax.ppermute(value, "gz", low_digit(step))

    small = [((64, 256), F32), ((64, 256), BF)]
    pay, cols, weight, own, low_geom, high_geom = prepare(
        features.reshape(8, 128, 256),
        fractions.transpose(0, 2, 3, 1, 4).reshape(2, 3, 4, 128),
        occupied.reshape(8, 1, 128),
        wave_index,
        radial_weight.T,
    )
    left, right = send(high_geom, "gx", 1), send(low_geom, "gx", 3)
    sent_pay = after(pay, left, right)
    far = lax.ppermute(sent_pay, "gz", far_pairs())
    near = send_low(sent_pay, 1)
    t0, t1, t2, t3, bt = call(
        structure_kernel,
        "structure",
        [((256, 256), BF), ((288, 256), BF), ((256, 256), BF), ((288, 256), BF)]
        + [((1024, 1024), BF)],
        [where, pay, cols, left, right],
        [((8, 128), F32), ((1024, 256), F32)],
        1,
    )
    t1, t2, t3 = after((t1, t2, t3), near)
    got = tuple(send(t, "gy", s) for s, t in ((1, t1), (2, t2), (3, t3)))
    inside = own_messages(after(pay, t1), own, weight)
    got = after(got, inside)
    u0, u1, u2, u3, home = call(
        first_sum_kernel,
        "first_sum",
        [((64, 256), F32)] + [((64, 256), BF)] * 3 + [((24, 128, 8), F32)],
        [t0, *got, own, left, right],
    )
    got = tuple(send_high(u, s) for s, u in ((1, u1), (2, u2), (3, u3)))
    side = plane_messages(where, pay, home, weight, None, BORDER_X, 0, "pair_side_own")
    got = after(got, side)
    sums, sent = call(more_sum_kernel, "second_sum", small, [u0, *got])
    got = send_low(sent, 1)
    side, inside = near_messages(where, after(near, sent), home, weight, side, inside)
    got = after(got, side, far)
    sums, sent = call(more_sum_kernel, "third_sum", small, [sums, got])
    got = tuple(send(sent, "gx", s) for s in (1, 2, 3))
    low, high = far_side_messages(where, after(far, sent), home, weight, side)
    got = after(got, low)
    sums, sent = call(more_sum_kernel, "fourth_sum", small, [sums, *got])
    got = send_low(sent, 2)
    inside = plane_messages(
        where, after(far, sent), home, weight, inside, INSIDE, 2, "pair_inside_far"
    )
    got = after(got, inside)
    low, high = after((low, high), got)
    x1, x3 = send(high, "gx", 1), send(low, "gx", 3)
    rows = call(
        filter_kernel,
        "filter",
        [((64, 256), BF)],
        [where, sums, got, ewald_mix, cols],
        (),
        1,
    )[0]
    got = tuple(send_high(rows, s) for s in (1, 2, 3))
    border = border_messages(where, pay, near, after(far, rows), home, weight)
    got = after(got, border)
    rows = jnp.concatenate([rows, *got], axis=0)
    got = tuple(send(rows, "gy", s) for s in (1, 2, 3))
    joined = call(
        ewald_kernel,
        "ewald",
        [((1024, 256), F32)],
        [where, bt, rows, *got, ewald_weight],
        [((1024, 256), BF)],
        1,
    )[0]
    x1, x3 = after((x1, x3), border)
    p1, p3 = call(border_sum_kernel, "border_sum", [((256, 256), BF)] * 2, [border, x1, x3])
    q1, q3 = send(p1, "gy", 1), send(p3, "gy", 3)
    q1, q3 = after((q1, q3), joined)
    out = call(
        update_kernel,
        "update",
        [((8, 128, 256), BF)],
        [joined, q1, q3, inside, x1, x3, pay, own, msg_weight, out_weight],
        (),
        0,
        12,
    )[0]
    return out.reshape(features.shape)


def solution(mesh):
    in_specs = (
        P("gx", "gy", "gz", None, None),
        P("gx", "gy", "gz", None, None),
        P("gx", "gy", "gz", None),
        P(),
        P(),
        P(),
        P(),
        P(),
        P(),
    )
    out_specs = P("gx", "gy", "gz", None, None)
    return jax.shard_map(body, mesh=mesh, in_specs=in_specs, out_specs=out_specs, check_vma=False)
```
